128 devices in a mesh: dp: 128 (over x, y, z, core).
Axes of the slice: x: 4, y: 4, z: 4, core: 2. Of those that a mesh axis runs over, the one named last changes fastest.
Arguments:
- query_emb: bfloat16 [16384, 1024], P('dp'), may hold values from -0.1875 to 0.1875
- doc_emb: bfloat16 [16384, 1024], P('dp'), may hold values from -0.1875 to 0.1875
- pair_blocks: int32 [128, 4, 2], replicated, may hold values from 0 to 127, as said below
- active_pair_count: int32 [128], replicated, may hold values from 0 to 4, as said below
Outputs:
- grad_query: float32 [16384, 1024], P('dp')
- grad_doc: float32 [16384, 1024], P('dp')
The draws below stay inside these ranges and needn't reach their ends.
Inputs may be any that keep to these rules, and one draw needn't show every extreme that they name: `pair_blocks`: the live slots of all owners together name every row block exactly 2 times as a row block, never pair a block with itself, and never repeat a tile; slots that are not live hold arbitrary block indices. `active_pair_count`: the counts sum to 256, and some owner has 4.
All inputs are finite; a program needn't handle non-finite values.
Results may differ from the reference program's by a relative error of at most 0.005.
Values may be sent and summed in bfloat16 or wider, within the bound.
No kernel may reach another device: no remote copies, remote signals or barrier semaphores. Data moves between devices by JAX's collectives and lax.ppermute only.
A program may use at most 64 MiB of HBM per device.

```python
import jax
import jax.numpy as jnp
from jax import lax

D = 1024
ROWS_DEV = 128
MEAN = 2
SLOTS = 4
BLOCKS = 128
ROWS = 16384


def plan_tables(key):
    base_key = jax.random.fold_in(key, 4242)
    key_list = jax.random.split(base_key, 5)
    offset_keys = jax.random.split(key_list[0], BLOCKS)
    offsets = jax.vmap(lambda single: jax.random.permutation(single, BLOCKS - 1)[:MEAN] + 1)(offset_keys)
    row_block = jnp.repeat(jnp.arange(BLOCKS, dtype=jnp.int32), MEAN)
    col_block = ((row_block.reshape(BLOCKS, MEAN) + offsets.astype(jnp.int32)) % BLOCKS).reshape(-1)
    shuffle = jax.random.permutation(key_list[1], BLOCKS * MEAN)
    row_block = row_block[shuffle]
    col_block = col_block[shuffle]
    owners = jax.random.permutation(key_list[2], BLOCKS)
    shifted = jax.random.randint(key_list[3], (BLOCKS // 2,), 0, MEAN + 1, dtype=jnp.int32).at[0].set(MEAN)
    counts = jnp.zeros((BLOCKS,), jnp.int32).at[owners[0::2]].set(MEAN + shifted).at[owners[1::2]].set(MEAN - shifted)
    count_ends = jnp.cumsum(counts).astype(jnp.int32)
    position = jnp.arange(BLOCKS * MEAN, dtype=jnp.int32)
    owner_of = jnp.searchsorted(count_ends, position, side='right').astype(jnp.int32)
    slot_of = position - (count_ends - counts)[owner_of]
    pair_table = jax.random.randint(key_list[4], (BLOCKS, SLOTS, 2), 0, BLOCKS, dtype=jnp.int32)
    pair_table = pair_table.at[owner_of, slot_of].set(jnp.stack([row_block, col_block], axis=1))
    return (pair_table, counts)


def draw_pair_blocks(key, part):
    return plan_tables(key)[0]


def draw_active_pair_count(key, part):
    return plan_tables(key)[1]


def shard_levels(rng, shape, cuts, least, top_value):
    def one(axis_at, parts):
        draws = jax.random.uniform(jax.random.fold_in(jax.random.fold_in(rng, 6), axis_at), (parts,), jnp.float32, least / len(cuts), top_value / len(cuts))
        return jnp.repeat(jnp.exp(draws), shape[axis_at] // parts).reshape((-1,) + (1,) * (len(shape) - axis_at - 1))

    level = one(*cuts[0])
    for cut in cuts[1:]:
        level = level * one(*cut)
    return level


def gaussian(stream_key, shape, deviation, limit, cuts=(), held_as=jnp.bfloat16):
    array = deviation * jax.random.normal(stream_key, shape, jnp.float32)
    if cuts:
        array = array * shard_levels(stream_key, shape, cuts, -0.22, 0.18)
    return jnp.clip(array, -limit, limit).astype(held_as)


def setup_inputs(seed: int = 0) -> dict:
    streams_of = jax.random.split(jax.random.key(seed), 5)
    return {
        "query_emb": gaussian(streams_of[0], (ROWS, D), 0.03125, 0.1875, ((0, 128),)),
        "doc_emb": gaussian(streams_of[1], (ROWS, D), 0.03125, 0.1875, ((0, 128),)),
        "pair_blocks": draw_pair_blocks(jax.random.fold_in(streams_of[4], 71), 0),
        "active_pair_count": draw_active_pair_count(jax.random.fold_in(streams_of[4], 71), 0),
    }


LOGIT_SCALE = 64.0
EPSILON = 1e-06

def unit_rows(raw_rows):
    widened = raw_rows.astype(jnp.float32)
    inverse = lax.rsqrt(lax.optimization_barrier(jnp.sum(widened * widened, axis=1)) + EPSILON)
    return (widened, inverse, (widened * inverse[:, None]).astype(jnp.bfloat16))

def unit_grad(widened, inverse, upstream):
    radial = lax.optimization_barrier(jnp.sum(widened * upstream, axis=1))
    return upstream * inverse[:, None] - widened * (radial * inverse * inverse * inverse)[:, None]

def reference(query_emb, doc_emb, pair_blocks, active_pair_count):
    query_wide, query_inverse, query_unit = unit_rows(query_emb)
    doc_wide, doc_inverse, doc_unit = unit_rows(doc_emb)
    query_blocks = query_unit.reshape(BLOCKS, ROWS_DEV, D)
    doc_blocks = doc_unit.reshape(BLOCKS, ROWS_DEV, D)
    tile_rows = pair_blocks[:, :, 0].reshape(-1).astype(jnp.int32)
    tile_cols = pair_blocks[:, :, 1].reshape(-1).astype(jnp.int32)
    tile_live = (jnp.arange(SLOTS, dtype=jnp.int32)[None, :] < active_pair_count[:, None]).reshape(-1).astype(jnp.float32)
    block_list = jnp.arange(BLOCKS, dtype=jnp.int32)

    def tile_scores(row_block, col_block):
        return LOGIT_SCALE * jnp.dot(query_blocks[row_block], doc_blocks[col_block].T, preferred_element_type=jnp.float32)

    def own_totals(block_index):
        exponentials = jnp.exp(tile_scores(block_index, block_index))
        return (lax.optimization_barrier(jnp.sum(exponentials, axis=1)), lax.optimization_barrier(jnp.sum(exponentials, axis=0)))
    row_total, col_total = lax.map(own_totals, block_list)

    def add_totals(totals, tile_item):
        row_block, col_block, alive_flag = tile_item
        exponentials = jnp.exp(tile_scores(row_block, col_block))
        row_acc = totals[0].at[row_block].add(alive_flag * lax.optimization_barrier(jnp.sum(exponentials, axis=1)))
        col_acc = totals[1].at[col_block].add(alive_flag * lax.optimization_barrier(jnp.sum(exponentials, axis=0)))
        return ((row_acc, col_acc), None)
    (row_total, col_total), unused = lax.scan(add_totals, (row_total, col_total), (tile_rows, tile_cols, tile_live))
    row_lse = jnp.log(row_total)
    col_lse = jnp.log(col_total)

    def tile_weight(row_block, col_block):
        scores = tile_scores(row_block, col_block)
        return 0.5 * (jnp.exp(scores - row_lse[row_block][:, None]) + jnp.exp(scores - col_lse[col_block][None, :]))

    def own_grads(block_index):
        weight = (tile_weight(block_index, block_index) - jnp.eye(ROWS_DEV, dtype=jnp.float32)).astype(jnp.bfloat16)
        query_part = (LOGIT_SCALE * jnp.dot(weight, doc_blocks[block_index], preferred_element_type=jnp.float32)).astype(jnp.bfloat16)
        doc_part = (LOGIT_SCALE * jnp.dot(weight.T, query_blocks[block_index], preferred_element_type=jnp.float32)).astype(jnp.bfloat16)
        return (query_part.astype(jnp.float32), doc_part.astype(jnp.float32))
    query_grad, doc_grad = lax.map(own_grads, block_list)

    def combine_gradients(grads, tile_item):
        row_block, col_block, alive_flag = tile_item
        weight = tile_weight(row_block, col_block).astype(jnp.bfloat16)
        query_part = (LOGIT_SCALE * jnp.dot(weight, doc_blocks[col_block], preferred_element_type=jnp.float32)).astype(jnp.bfloat16)
        doc_part = (LOGIT_SCALE * jnp.dot(weight.T, query_blocks[row_block], preferred_element_type=jnp.float32)).astype(jnp.bfloat16)
        query_running_total = grads[0].at[row_block].add(alive_flag * query_part.astype(jnp.float32))
        doc_acc = grads[1].at[col_block].add(alive_flag * doc_part.astype(jnp.float32))
        return ((query_running_total, doc_acc), None)
    (query_grad, doc_grad), unused = lax.scan(combine_gradients, (query_grad, doc_grad), (tile_rows, tile_cols, tile_live))
    grad_query = unit_grad(query_wide, query_inverse, query_grad.reshape(ROWS, D))
    grad_doc = unit_grad(doc_wide, doc_inverse, doc_grad.reshape(ROWS, D))
    return (grad_query, grad_doc)
```

```python
import jax
import jax.numpy as jnp
from jax import lax
from jax.experimental import pallas as pl
from jax.experimental.pallas import tpu as pltpu
from jax.sharding import PartitionSpec as P

LOGIT_SCALE = 64.0
EPSILON = 1e-06
LANES = 128
SUB = 8


def whole(space):
    return pl.BlockSpec(memory_space=space)


def vmem_call(body, outs, n_smem, n_vmem, scratch=(), name=None):
    return pl.pallas_call(
        body,
        out_shape=outs,
        in_specs=[whole(pltpu.SMEM)] * n_smem + [whole(pltpu.VMEM)] * n_vmem,
        out_specs=jax.tree.map(lambda _: whole(pltpu.VMEM), outs),
        scratch_shapes=list(scratch),
        name=name,
    )


def inverse_norm(wide):
    return lax.rsqrt(jnp.sum(wide * wide, axis=1, keepdims=True) + EPSILON)


def from_pieces(pieces, slot):
    row_tiles, col_tiles = pieces.shape[:2]
    return jnp.concatenate(
        [pieces[:, ct, slot].reshape(row_tiles * SUB, LANES) for ct in range(col_tiles)], axis=1
    )


def dot_nt(a, b):
    return lax.dot_general(a, b, (((1,), (1,)), ((), ())), preferred_element_type=jnp.float32)


def dot_tn(a, b):
    return lax.dot_general(a, b, (((0,), (0,)), ((), ())), preferred_element_type=jnp.float32)


def dot_nn(a, b):
    return lax.dot_general(a, b, (((1,), (0,)), ((), ())), preferred_element_type=jnp.float32)


def own_kernel(q_ref, d_ref, qu_ref, du_ref, inv_ref, et_ref):
    q_wide = q_ref[...].astype(jnp.float32)
    d_wide = d_ref[...].astype(jnp.float32)
    q_inv = inverse_norm(q_wide)
    d_inv = inverse_norm(d_wide)
    q = (q_wide * q_inv).astype(jnp.bfloat16)
    d = (d_wide * d_inv).astype(jnp.bfloat16)
    qu_ref[...] = q
    du_ref[...] = d
    lane = lax.broadcasted_iota(jnp.int32, inv_ref.shape, 1)
    inv_ref[...] = jnp.where(lane == 0, q_inv, d_inv)
    et_ref[...] = jnp.exp(LOGIT_SCALE * dot_nt(d, q))


def gather_kernel(cols_ref, spread_ref, out_ref):
    def step(dest, carry):
        first = spread_ref[cols_ref[2 * dest]]
        second = spread_ref[cols_ref[2 * dest + 1]]
        out_ref[dest, 0:SUB, :] = first
        out_ref[dest, SUB : 2 * SUB, :] = second
        return carry

    lax.fori_loop(0, out_ref.shape[0], step, 0, unroll=8)


def split_pair(value, odd):
    high = value.astype(jnp.bfloat16).astype(jnp.float32)
    return jnp.where(odd, value - high, high)


def tiles_kernel(qu_ref, et_own_ref, fetched_ref, send_ref, et_ref, row_ref, dk_ref):
    row_tiles, col_tiles = send_ref.shape[:2]
    q = qu_ref[...]
    pieces = fetched_ref[...].astype(jnp.float32)
    pieces = pieces.reshape(row_tiles, col_tiles, 2, SUB, LANES)
    et_own = et_own_ref[...]
    row_total = jnp.sum(et_own, axis=0, keepdims=True)
    col_own = jnp.sum(et_own, axis=1, keepdims=True)
    ets, cols = [], []
    for k in range(2):
        wide = from_pieces(pieces, k)
        unit = (wide * inverse_norm(wide)).astype(jnp.bfloat16)
        dk_ref[k] = unit
        et = jnp.exp(LOGIT_SCALE * dot_nt(unit, q))
        et_ref[k] = et
        row_total = row_total + jnp.sum(et, axis=0, keepdims=True)
        cols.append(jnp.sum(et, axis=1, keepdims=True))
        ets.append(et)
    row_ref[...] = row_total
    row_inv = 1.0 / row_total
    half = 0.5 * LOGIT_SCALE
    parts = []
    for make in (lambda e: e * row_inv, lambda e: e):
        parts.append([half * dot_nn(make(e).astype(jnp.bfloat16), q) for e in ets])
    for ct in range(col_tiles):
        lanes = slice(ct * LANES, (ct + 1) * LANES)
        for kind in range(2):
            pair = [x[:, lanes].reshape(row_tiles, 1, SUB, LANES) for x in parts[kind]]
            both = jnp.concatenate(pair, axis=1).reshape(row_tiles, 2 * SUB, LANES)
            send_ref[:, ct, 2 * SUB * kind : 2 * SUB * (kind + 1), :] = both.astype(jnp.bfloat16)
    rows = row_tiles * SUB
    lane = lax.broadcasted_iota(jnp.int32, (rows, LANES), 1)
    value = jnp.where(lane < 2, col_own, jnp.where(lane < 4, cols[0], cols[1]))
    scalars = split_pair(value, lane % 2 == 1).reshape(row_tiles, SUB, LANES).astype(jnp.bfloat16)
    for ct in range(col_tiles):
        send_ref[:, ct, 4 * SUB :, :] = scalars


def combine_kernel(cols_ref, recv_ref, out_ref, acc_a, acc_b, acc_t):
    blocks = recv_ref.shape[0]
    acc_a[...] = jnp.zeros_like(acc_a)
    acc_b[...] = jnp.zeros_like(acc_b)
    lane3 = lax.broadcasted_iota(jnp.int32, acc_t.shape, 2)
    own = recv_ref[:, 4 * SUB :, :].astype(jnp.float32)
    acc_t[...] = jnp.where(lane3 < 2, own, 0.0)
    lane = lax.broadcasted_iota(jnp.int32, (SUB, LANES), 1)
    masks = [(lane >= 2) & (lane < 4), (lane >= 4) & (lane < 6)]

    def add(source, carry):
        a = recv_ref[source, 0 : 2 * SUB, :].astype(jnp.float32)
        b = recv_ref[source, 2 * SUB : 4 * SUB, :].astype(jnp.float32)
        t = recv_ref[source, 4 * SUB :, :].astype(jnp.float32)
        for k in range(2):
            col = cols_ref[2 * source + k]
            acc_a[col] = acc_a[col] + a[k * SUB : (k + 1) * SUB]
            acc_b[col] = acc_b[col] + b[k * SUB : (k + 1) * SUB]
            acc_t[col] = acc_t[col] + jnp.where(masks[k], t, 0.0)
        return carry

    lax.fori_loop(0, blocks, add, 0, unroll=8)
    total = jnp.broadcast_to(jnp.sum(acc_t[...], axis=2, keepdims=True), acc_t.shape)
    acc_t[...] = total
    acc_a[...] = acc_a[...] + acc_b[...] / total
    odd = lane % 2 == 1

    def emit(dest, carry):
        value = jnp.where(
            lane < 2,
            acc_t[dest],
            jnp.where(lane < 4, acc_t[cols_ref[2 * dest]], acc_t[cols_ref[2 * dest + 1]]),
        )
        both = jnp.concatenate([acc_a[dest], split_pair(value, odd)], axis=0)
        out_ref[dest] = both.astype(jnp.bfloat16)
        return carry

    lax.fori_loop(0, blocks, emit, 0, unroll=8)


def unit_grad(wide, inverse, upstream):
    radial = jnp.sum(wide * upstream, axis=1, keepdims=True)
    return upstream * inverse - wide * (radial * inverse * inverse * inverse)


def final_kernel(
    q_ref, d_ref, qu_ref, du_ref, inv_ref, et_own_ref, et_ref, row_ref, dk_ref, home_ref, gq_ref, gd_ref
):
    rows, features = q_ref.shape
    row_tiles, col_tiles = rows // SUB, features // LANES
    pieces = home_ref[...].astype(jnp.float32).reshape(row_tiles, col_tiles, 2, SUB, LANES)
    scalars = pieces[:, 0, 1].reshape(rows, LANES)
    totals = [scalars[:, 2 * i : 2 * i + 1] + scalars[:, 2 * i + 1 : 2 * i + 2] for i in range(3)]
    row_inv = 1.0 / row_ref[...]

    def weight(et, total):
        return 0.5 * (et * row_inv + et * (1.0 / total))

    own = weight(et_own_ref[...], totals[0])
    diagonal = lax.broadcasted_iota(jnp.int32, own.shape, 0) == lax.broadcasted_iota(
        jnp.int32, own.shape, 1
    )
    own = (own - jnp.where(diagonal, 1.0, 0.0)).astype(jnp.bfloat16)

    def part(x):
        return (LOGIT_SCALE * x).astype(jnp.bfloat16).astype(jnp.float32)

    query = part(dot_tn(own, du_ref[...]))
    for k in range(2):
        w = weight(et_ref[k], totals[k + 1]).astype(jnp.bfloat16)
        query = query + part(dot_tn(w, dk_ref[k]))
    gq_ref[...] = unit_grad(q_ref[...].astype(jnp.float32), inv_ref[:, 0:1], query)
    doc = part(dot_nn(own, qu_ref[...])) + from_pieces(pieces, 0)
    gd_ref[...] = unit_grad(d_ref[...].astype(jnp.float32), inv_ref[:, 1:2], doc)


def exchange(x):
    return lax.all_to_all(x, "dp", split_axis=0, concat_axis=0, tiled=True)


def row_columns(pair_blocks, active_pair_count, blocks):
    slots = pair_blocks.shape[1]
    live = jnp.arange(slots)[None, :] < active_pair_count[:, None]
    rows = jnp.where(live, pair_blocks[:, :, 0], -1).reshape(1, -1)
    cols = pair_blocks[:, :, 1].reshape(1, -1)
    match = rows == jnp.arange(blocks)[:, None]
    low = jnp.min(jnp.where(match, cols, blocks - 1), axis=1)
    high = jnp.max(jnp.where(match, cols, 0), axis=1)
    return jnp.stack([low, high], axis=1).reshape(-1).astype(jnp.int32)


def on_device(query_emb, doc_emb, pair_blocks, active_pair_count):
    blocks = lax.axis_size("dp")
    rows, features = query_emb.shape
    row_tiles, col_tiles = rows // SUB, features // LANES
    assert row_tiles * col_tiles == blocks
    sds = jax.ShapeDtypeStruct
    bf16, f32 = jnp.bfloat16, jnp.float32

    doc_pieces = doc_emb.reshape(row_tiles, SUB, col_tiles, LANES).transpose(0, 2, 1, 3)
    spread = exchange(doc_pieces.reshape(blocks, SUB, LANES))
    cols = row_columns(pair_blocks, active_pair_count, blocks)
    qu, du, inv, et_own = vmem_call(
        own_kernel,
        (sds((rows, features), bf16), sds((rows, features), bf16), sds((rows, 2), f32), sds((rows, rows), f32)),
        0,
        2,
        name="own",
    )(query_emb, doc_emb)
    wanted = vmem_call(gather_kernel, sds((blocks, 2 * SUB, LANES), bf16), 1, 1, name="gather")(
        cols, spread
    )
    fetched = exchange(wanted)
    send, et, row_total, dk = vmem_call(
        tiles_kernel,
        (
            sds((row_tiles, col_tiles, 5 * SUB, LANES), bf16),
            sds((2, rows, rows), f32),
            sds((1, rows), f32),
            sds((2, rows, features), bf16),
        ),
        0,
        3,
        name="tiles",
    )(qu, et_own, fetched)
    parts = exchange(send.reshape(blocks, 5 * SUB, LANES))
    acc = pltpu.VMEM((blocks, SUB, LANES), f32)
    combined = vmem_call(
        combine_kernel, sds((blocks, 2 * SUB, LANES), bf16), 1, 1, (acc, acc, acc), name="combine"
    )(cols, parts)
    home = exchange(combined)
    return vmem_call(
        final_kernel, (sds((rows, features), f32), sds((rows, features), f32)), 0, 10, name="final"
    )(query_emb, doc_emb, qu, du, inv, et_own, et, row_total, dk, home)


def solution(mesh):
    return jax.shard_map(
        on_device,
        mesh=mesh,
        in_specs=(P("dp", None), P("dp", None), P(), P()),
        out_specs=(P("dp", None), P("dp", None)),
        check_vma=False,
    )
```

```python
import jax
import jax.numpy as jnp
from jax import lax
from jax.experimental import pallas as pl
from jax.experimental.pallas import tpu as pltpu
from jax.sharding import PartitionSpec as P

LOGIT_SCALE = 64.0
EPSILON = 1e-06
LANES = 128
SUB = 8
VMEM_BYTES = 16 * 1024 * 1024


def whole(space):
    return pl.BlockSpec(memory_space=space)


def vmem_call(body, outs, n_smem, n_vmem, scratch=(), name=None):
    call = pl.pallas_call(
        body,
        out_shape=outs,
        in_specs=[whole(pltpu.SMEM)] * n_smem + [whole(pltpu.VMEM)] * n_vmem,
        out_specs=jax.tree.map(lambda _: whole(pltpu.VMEM), outs),
        scratch_shapes=list(scratch),
        compiler_params=pltpu.CompilerParams(vmem_limit_bytes=VMEM_BYTES),
        name=name,
    )

    def run(*args):
        kept = [pltpu.with_memory_space_constraint(x, pltpu.VMEM) for x in args[n_smem:]]
        return call(*args[:n_smem], *kept)

    return run


def inverse_norm(wide):
    return lax.rsqrt(jnp.sum(wide * wide, axis=1, keepdims=True) + EPSILON)


def from_pieces(pieces, slot):
    row_tiles, col_tiles = pieces.shape[:2]
    return jnp.concatenate(
        [pieces[:, ct, slot].reshape(row_tiles * SUB, LANES) for ct in range(col_tiles)], axis=1
    )


def dot_nt(a, b):
    return lax.dot_general(a, b, (((1,), (1,)), ((), ())), preferred_element_type=jnp.float32)


def dot_tn(a, b):
    return lax.dot_general(a, b, (((0,), (0,)), ((), ())), preferred_element_type=jnp.float32)


def dot_nn(a, b):
    return lax.dot_general(a, b, (((1,), (0,)), ((), ())), preferred_element_type=jnp.float32)


def own_kernel(q_ref, d_ref, qu_ref, du_ref, inv_ref, et_ref):
    q_wide = q_ref[...].astype(jnp.float32)
    d_wide = d_ref[...].astype(jnp.float32)
    q_inv = inverse_norm(q_wide)
    d_inv = inverse_norm(d_wide)
    q = (q_wide * q_inv).astype(jnp.bfloat16)
    d = (d_wide * d_inv).astype(jnp.bfloat16)
    qu_ref[...] = q
    du_ref[...] = d
    lane = lax.broadcasted_iota(jnp.int32, inv_ref.shape, 1)
    inv_ref[...] = jnp.where(lane == 0, q_inv, d_inv)
    et_ref[...] = jnp.exp(LOGIT_SCALE * dot_nt(d, q))


def gather_kernel(cols_ref, spread_ref, out_ref):
    def step(dest, carry):
        first = spread_ref[cols_ref[2 * dest]]
        second = spread_ref[cols_ref[2 * dest + 1]]
        out_ref[dest, 0:SUB, :] = first
        out_ref[dest, SUB : 2 * SUB, :] = second
        return carry

    lax.fori_loop(0, out_ref.shape[0], step, 0, unroll=8)


def split_pair(value, odd):
    high = value.astype(jnp.bfloat16).astype(jnp.float32)
    return jnp.where(odd, value - high, high)


def tiles_kernel(qu_ref, et_own_ref, fetched_ref, send_ref, et_ref, row_ref, dk_ref):
    row_tiles, col_tiles = send_ref.shape[:2]
    q = qu_ref[...]
    pieces = fetched_ref[...].astype(jnp.float32)
    pieces = pieces.reshape(row_tiles, col_tiles, 2, SUB, LANES)
    et_own = et_own_ref[...]
    row_total = jnp.sum(et_own, axis=0, keepdims=True)
    col_own = jnp.sum(et_own, axis=1, keepdims=True)
    ets, cols = [], []
    for k in range(2):
        wide = from_pieces(pieces, k)
        unit = (wide * inverse_norm(wide)).astype(jnp.bfloat16)
        dk_ref[k] = unit
        et = jnp.exp(LOGIT_SCALE * dot_nt(unit, q))
        et_ref[k] = et
        row_total = row_total + jnp.sum(et, axis=0, keepdims=True)
        cols.append(jnp.sum(et, axis=1, keepdims=True))
        ets.append(et)
    row_ref[...] = row_total
    row_inv = 1.0 / row_total
    half = 0.5 * LOGIT_SCALE
    parts = []
    for make in (lambda e: e * row_inv, lambda e: e):
        parts.append([half * dot_nn(make(e).astype(jnp.bfloat16), q) for e in ets])
    for ct in range(col_tiles):
        lanes = slice(ct * LANES, (ct + 1) * LANES)
        for kind in range(2):
            pair = [x[:, lanes].reshape(row_tiles, 1, SUB, LANES) for x in parts[kind]]
            both = jnp.concatenate(pair, axis=1).reshape(row_tiles, 2 * SUB, LANES)
            send_ref[:, ct, 2 * SUB * kind : 2 * SUB * (kind + 1), :] = both.astype(jnp.bfloat16)
    rows = row_tiles * SUB
    lane = lax.broadcasted_iota(jnp.int32, (rows, LANES), 1)
    value = jnp.where(lane < 2, col_own, jnp.where(lane < 4, cols[0], cols[1]))
    scalars = split_pair(value, lane % 2 == 1).reshape(row_tiles, SUB, LANES).astype(jnp.bfloat16)
    for ct in range(col_tiles):
        send_ref[:, ct, 4 * SUB :, :] = scalars


def combine_kernel(cols_ref, recv_ref, out_ref, acc_a, acc_b, acc_t):
    blocks = recv_ref.shape[0]
    acc_a[...] = jnp.zeros_like(acc_a)
    acc_b[...] = jnp.zeros_like(acc_b)
    lane3 = lax.broadcasted_iota(jnp.int32, acc_t.shape, 2)
    own = recv_ref[:, 4 * SUB :, :].astype(jnp.float32)
    acc_t[...] = jnp.where(lane3 < 2, own, 0.0)
    lane = lax.broadcasted_iota(jnp.int32, (SUB, LANES), 1)
    masks = [(lane >= 2) & (lane < 4), (lane >= 4) & (lane < 6)]

    def add(source, carry):
        a = recv_ref[source, 0 : 2 * SUB, :].astype(jnp.float32)
        b = recv_ref[source, 2 * SUB : 4 * SUB, :].astype(jnp.float32)
        t = recv_ref[source, 4 * SUB :, :].astype(jnp.float32)
        for k in range(2):
            col = cols_ref[2 * source + k]
            acc_a[col] = acc_a[col] + a[k * SUB : (k + 1) * SUB]
            acc_b[col] = acc_b[col] + b[k * SUB : (k + 1) * SUB]
            acc_t[col] = acc_t[col] + jnp.where(masks[k], t, 0.0)
        return carry

    lax.fori_loop(0, blocks, add, 0, unroll=8)
    total = jnp.broadcast_to(jnp.sum(acc_t[...], axis=2, keepdims=True), acc_t.shape)
    acc_t[...] = total
    acc_a[...] = acc_a[...] + acc_b[...] / total
    odd = lane % 2 == 1

    def emit(dest, carry):
        value = jnp.where(
            lane < 2,
            acc_t[dest],
            jnp.where(lane < 4, acc_t[cols_ref[2 * dest]], acc_t[cols_ref[2 * dest + 1]]),
        )
        both = jnp.concatenate([acc_a[dest], split_pair(value, odd)], axis=0)
        out_ref[dest] = both.astype(jnp.bfloat16)
        return carry

    lax.fori_loop(0, blocks, emit, 0, unroll=8)


def unit_grad(wide, inverse, upstream):
    radial = jnp.sum(wide * upstream, axis=1, keepdims=True)
    return upstream * inverse - wide * (radial * inverse * inverse * inverse)


def final_kernel(
    q_ref, d_ref, qu_ref, du_ref, inv_ref, et_own_ref, et_ref, row_ref, dk_ref, home_ref, gq_ref, gd_ref
):
    rows, features = q_ref.shape
    row_tiles, col_tiles = rows // SUB, features // LANES
    pieces = home_ref[...].astype(jnp.float32).reshape(row_tiles, col_tiles, 2, SUB, LANES)
    scalars = pieces[:, 0, 1].reshape(rows, LANES)
    totals = [scalars[:, 2 * i : 2 * i + 1] + scalars[:, 2 * i + 1 : 2 * i + 2] for i in range(3)]
    row_inv = 1.0 / row_ref[...]

    def weight(et, total):
        return 0.5 * (et * row_inv + et * (1.0 / total))

    own = weight(et_own_ref[...], totals[0])
    diagonal = lax.broadcasted_iota(jnp.int32, own.shape, 0) == lax.broadcasted_iota(
        jnp.int32, own.shape, 1
    )
    own = (own - jnp.where(diagonal, 1.0, 0.0)).astype(jnp.bfloat16)

    def part(x):
        return (LOGIT_SCALE * x).astype(jnp.bfloat16).astype(jnp.float32)

    query = part(dot_tn(own, du_ref[...]))
    for k in range(2):
        w = weight(et_ref[k], totals[k + 1]).astype(jnp.bfloat16)
        query = query + part(dot_tn(w, dk_ref[k]))
    gq_ref[...] = unit_grad(q_ref[...].astype(jnp.float32), inv_ref[:, 0:1], query)
    doc = part(dot_nn(own, qu_ref[...])) + from_pieces(pieces, 0)
    gd_ref[...] = unit_grad(d_ref[...].astype(jnp.float32), inv_ref[:, 1:2], doc)


def exchange(x):
    return lax.all_to_all(x, "dp", split_axis=0, concat_axis=0, tiled=True)


def row_columns(pair_blocks, active_pair_count, blocks):
    slots = pair_blocks.shape[1]
    live = jnp.arange(slots)[None, :] < active_pair_count[:, None]
    rows = jnp.where(live, pair_blocks[:, :, 0], -1).reshape(1, -1)
    cols = pair_blocks[:, :, 1].reshape(1, -1)
    match = rows == jnp.arange(blocks)[:, None]
    low = jnp.min(jnp.where(match, cols, blocks - 1), axis=1)
    high = jnp.max(jnp.where(match, cols, 0), axis=1)
    return jnp.stack([low, high], axis=1).reshape(-1).astype(jnp.int32)


def on_device(query_emb, doc_emb, pair_blocks, active_pair_count):
    blocks = lax.axis_size("dp")
    rows, features = query_emb.shape
    row_tiles, col_tiles = rows // SUB, features // LANES
    assert row_tiles * col_tiles == blocks
    sds = pltpu.VMEM
    bf16, f32 = jnp.bfloat16, jnp.float32

    doc_pieces = doc_emb.reshape(row_tiles, SUB, col_tiles, LANES).transpose(0, 2, 1, 3)
    spread = exchange(doc_pieces.reshape(blocks, SUB, LANES))
    cols = row_columns(pair_blocks, active_pair_count, blocks)
    qu, du, inv, et_own = vmem_call(
        own_kernel,
        (sds((rows, features), bf16), sds((rows, features), bf16), sds((rows, 2), f32), sds((rows, rows), f32)),
        0,
        2,
        name="own",
    )(query_emb, doc_emb)
    wanted = vmem_call(gather_kernel, sds((blocks, 2 * SUB, LANES), bf16), 1, 1, name="gather")(
        cols, spread
    )
    fetched = exchange(wanted)
    send, et, row_total, dk = vmem_call(
        tiles_kernel,
        (
            sds((row_tiles, col_tiles, 5 * SUB, LANES), bf16),
            sds((2, rows, rows), f32),
            sds((1, rows), f32),
            sds((2, rows, features), bf16),
        ),
        0,
        3,
        name="tiles",
    )(qu, et_own, fetched)
    parts = exchange(send.reshape(blocks, 5 * SUB, LANES))
    acc = pltpu.VMEM((blocks, SUB, LANES), f32)
    combined = vmem_call(
        combine_kernel, sds((blocks, 2 * SUB, LANES), bf16), 1, 1, (acc, acc, acc), name="combine"
    )(cols, parts)
    home = exchange(combined)
    return vmem_call(
        final_kernel, (jax.ShapeDtypeStruct((rows, features), f32), jax.ShapeDtypeStruct((rows, features), f32)), 0, 10, name="final"
    )(query_emb, doc_emb, qu, du, inv, et_own, et, row_total, dk, home)


def solution(mesh):
    return jax.shard_map(
        on_device,
        mesh=mesh,
        in_specs=(P("dp", None), P("dp", None), P(), P()),
        out_specs=(P("dp", None), P("dp", None)),
        check_vma=False,
    )
```

```python
import jax
import jax.numpy as jnp
from jax import lax
from jax.experimental import pallas as pl
from jax.experimental.pallas import tpu as pltpu
from jax.sharding import PartitionSpec as P

LOGIT_SCALE = 64.0
EPSILON = 1e-06
LANES = 128
SUB = 8
PIECE = 16
VMEM_BYTES = 16 * 1024 * 1024
BF16 = jnp.bfloat16
F32 = jnp.float32


def vmem_call(body, outs, n_smem, n_vmem, scratch=(), name=None):
    spaces = [pltpu.SMEM] * n_smem + [pltpu.VMEM] * n_vmem
    call = pl.pallas_call(
        body,
        out_shape=outs,
        in_specs=[pl.BlockSpec(memory_space=space) for space in spaces],
        out_specs=jax.tree.map(lambda _: pl.BlockSpec(memory_space=pltpu.VMEM), outs),
        scratch_shapes=list(scratch),
        compiler_params=pltpu.CompilerParams(vmem_limit_bytes=VMEM_BYTES),
        name=name,
    )

    def run(*args):
        kept = [pltpu.with_memory_space_constraint(x, pltpu.VMEM) for x in args[n_smem:]]
        return call(*args[:n_smem], *kept)

    return run


def inverse_norm(wide):
    return lax.rsqrt(jnp.sum(wide * wide, axis=1, keepdims=True) + EPSILON)


def from_pieces(pieces, first):
    row_tiles, pairs = pieces.shape[:2]
    chunks = []
    for pair in range(pairs):
        for half in range(PIECE // SUB):
            at = first + half * SUB
            chunks.append(pieces[:, pair, at : at + SUB].reshape(row_tiles * SUB, LANES))
    return jnp.concatenate(chunks, axis=1)


def dot_nt(a, b):
    return lax.dot_general(a, b, (((1,), (1,)), ((), ())), preferred_element_type=F32)


def dot_tn(a, b):
    return lax.dot_general(a, b, (((0,), (0,)), ((), ())), preferred_element_type=F32)


def dot_nn(a, b):
    return lax.dot_general(a, b, (((1,), (0,)), ((), ())), preferred_element_type=F32)


def own_kernel(q_ref, d_ref, qu_ref, du_ref, inv_ref, et_ref):
    q_wide = q_ref[...].astype(F32)
    d_wide = d_ref[...].astype(F32)
    q_inv = inverse_norm(q_wide)
    d_inv = inverse_norm(d_wide)
    q = (q_wide * q_inv).astype(BF16)
    d = (d_wide * d_inv).astype(BF16)
    qu_ref[...] = q
    du_ref[...] = d
    lane = lax.broadcasted_iota(jnp.int32, inv_ref.shape, 1)
    inv_ref[...] = jnp.where(lane == 0, q_inv, d_inv)
    et_ref[...] = jnp.exp(LOGIT_SCALE * dot_nt(d, q))


def gather_kernel(cols_ref, mine_ref, other_ref, out_ref):
    chips = out_ref.shape[0]

    def step(dest, carry):
        for k in range(2):
            col = cols_ref[2 * dest + k]
            chip = lax.rem(col, chips)
            block = jnp.where(col < chips, mine_ref[chip], other_ref[chip])
            out_ref[dest, k * PIECE : (k + 1) * PIECE, :] = block
        return carry

    lax.fori_loop(0, chips, step, 0, unroll=8)


def split_pair(value, odd):
    high = value.astype(BF16).astype(F32)
    return jnp.where(odd, value - high, high)


def tiles_kernel(qu_ref, et_own_ref, fetched_ref, send_ref, et_ref, row_ref, dk_ref):
    row_tiles, pairs = send_ref.shape[:2]
    q = qu_ref[...]
    pieces = fetched_ref[...].astype(F32).reshape(row_tiles, pairs, 2 * PIECE, LANES)
    et_own = et_own_ref[...]
    row_total = jnp.sum(et_own, axis=0, keepdims=True)
    col_own = jnp.sum(et_own, axis=1, keepdims=True)
    ets, cols = [], []
    for k in range(2):
        wide = from_pieces(pieces, k * PIECE)
        unit = (wide * inverse_norm(wide)).astype(BF16)
        dk_ref[k] = unit
        et = jnp.exp(LOGIT_SCALE * dot_nt(unit, q))
        et_ref[k] = et
        row_total = row_total + jnp.sum(et, axis=0, keepdims=True)
        cols.append(jnp.sum(et, axis=1, keepdims=True))
        ets.append(et)
    row_ref[...] = row_total
    row_inv = 1.0 / row_total
    half = 0.5 * LOGIT_SCALE
    at = 0
    for make in (lambda e: e * row_inv, lambda e: e):
        for et in ets:
            part = half * dot_nn(make(et).astype(BF16), q)
            for pair in range(pairs):
                lanes = pair * 2 * LANES
                both = [
                    part[:, lanes + h * LANES : lanes + (h + 1) * LANES].reshape(row_tiles, 1, SUB, LANES)
                    for h in range(2)
                ]
                both = jnp.concatenate(both, axis=1).reshape(row_tiles, PIECE, LANES)
                send_ref[:, pair, at : at + PIECE, :] = both.astype(BF16)
            at += PIECE
    lane = lax.broadcasted_iota(jnp.int32, (row_tiles * SUB, LANES), 1)
    value = jnp.where(lane < 2, col_own, jnp.where(lane < 4, cols[0], cols[1]))
    scalars = split_pair(value, lane % 2 == 1).reshape(row_tiles, SUB, LANES).astype(BF16)
    for pair in range(pairs):
        send_ref[:, pair, at:, :] = scalars


def add_kernel(cols_ref, recv_ref, swap_ref, acc_a, acc_b, acc_t):
    chips = recv_ref.shape[0]
    acc_a[...] = jnp.zeros_like(acc_a)
    acc_b[...] = jnp.zeros_like(acc_b)
    lane3 = lax.broadcasted_iota(jnp.int32, (chips, SUB, LANES), 2)
    acc_t[0:chips] = jnp.where(lane3 < 2, recv_ref[:, 4 * PIECE :, :].astype(F32), 0.0)
    acc_t[chips:] = jnp.zeros((chips, SUB, LANES), F32)
    lane = lax.broadcasted_iota(jnp.int32, (SUB, LANES), 1)
    masks = [(lane >= 2) & (lane < 4), (lane >= 4) & (lane < 6)]

    def add(source, carry):
        t = recv_ref[source, 4 * PIECE :, :].astype(F32)
        for k in range(2):
            col = cols_ref[2 * source + k]
            a = recv_ref[source, k * PIECE : (k + 1) * PIECE, :].astype(F32)
            b = recv_ref[source, (k + 2) * PIECE : (k + 3) * PIECE, :].astype(F32)
            acc_a[col] = acc_a[col] + a
            acc_b[col] = acc_b[col] + b
            acc_t[col] = acc_t[col] + jnp.where(masks[k], t, 0.0)
        return carry

    lax.fori_loop(0, chips, add, 0, unroll=8)
    total = jnp.broadcast_to(jnp.sum(acc_t[...], axis=2, keepdims=True), acc_t.shape)
    acc_t[...] = total
    swap_ref[:, 0:PIECE, :] = acc_a[chips:].astype(BF16)
    swap_ref[:, PIECE : 2 * PIECE, :] = acc_b[chips:].astype(BF16)
    odd = lax.broadcasted_iota(jnp.int32, total.shape, 2) % 2 == 1
    pair = split_pair(total, odd).astype(BF16)
    swap_ref[:, 2 * PIECE : 2 * PIECE + SUB, :] = pair[chips:]
    swap_ref[:, 2 * PIECE + SUB :, :] = pair[:chips]


def finish_kernel(cols_ref, swap_ref, acc_a, acc_b, acc_t, out_ref, total_ref):
    chips = out_ref.shape[0]
    lane3 = lax.broadcasted_iota(jnp.int32, (chips, SUB, LANES), 2)

    def total_of(at, mine):
        pair = jnp.where(lane3 < 2, swap_ref[:, at : at + SUB, :].astype(F32), 0.0)
        return mine + jnp.broadcast_to(jnp.sum(pair, axis=2, keepdims=True), mine.shape)

    own_total = total_of(2 * PIECE, acc_t[0:chips])
    total_ref[0:chips] = own_total
    total_ref[chips:] = total_of(2 * PIECE + SUB, acc_t[chips:])
    inverse = 1.0 / own_total
    inverse = jnp.concatenate([inverse[:, None], inverse[:, None]], axis=1).reshape(chips, PIECE, LANES)
    a = acc_a[0:chips] + swap_ref[:, 0:PIECE, :].astype(F32)
    b = acc_b[0:chips] + swap_ref[:, PIECE : 2 * PIECE, :].astype(F32)
    out_ref[:, 0:PIECE, :] = (a + b * inverse).astype(BF16)
    lane = lax.broadcasted_iota(jnp.int32, (SUB, LANES), 1)
    odd = lane % 2 == 1

    def emit(dest, carry):
        value = jnp.where(
            lane < 2,
            total_ref[dest],
            jnp.where(lane < 4, total_ref[cols_ref[2 * dest]], total_ref[cols_ref[2 * dest + 1]]),
        )
        out_ref[dest, PIECE:, :] = split_pair(value, odd).astype(BF16)
        return carry

    lax.fori_loop(0, chips, emit, 0, unroll=8)


def unit_grad(wide, inverse, upstream):
    radial = jnp.sum(wide * upstream, axis=1, keepdims=True)
    return upstream * inverse - wide * (radial * inverse * inverse * inverse)


def final_kernel(
    q_ref, d_ref, qu_ref, du_ref, inv_ref, et_own_ref, et_ref, row_ref, dk_ref, home_ref, gq_ref, gd_ref
):
    rows = q_ref.shape[0]
    row_tiles = rows // SUB
    pieces = home_ref[...].astype(F32)
    pieces = pieces.reshape(row_tiles, pieces.shape[0] // row_tiles, PIECE + SUB, LANES)
    scalars = pieces[:, 0, PIECE:].reshape(rows, LANES)
    totals = [scalars[:, 2 * i : 2 * i + 1] + scalars[:, 2 * i + 1 : 2 * i + 2] for i in range(3)]
    row_inv = 1.0 / row_ref[...]

    def weight(et, total):
        return 0.5 * (et * row_inv + et * (1.0 / total))

    own = weight(et_own_ref[...], totals[0])
    diagonal = lax.broadcasted_iota(jnp.int32, own.shape, 0) == lax.broadcasted_iota(
        jnp.int32, own.shape, 1
    )
    own = (own - jnp.where(diagonal, 1.0, 0.0)).astype(BF16)

    def part(x):
        return (LOGIT_SCALE * x).astype(BF16).astype(F32)

    query = part(dot_tn(own, du_ref[...]))
    for k in range(2):
        w = weight(et_ref[k], totals[k + 1]).astype(BF16)
        query = query + part(dot_tn(w, dk_ref[k]))
    gq_ref[...] = unit_grad(q_ref[...].astype(F32), inv_ref[:, 0:1], query)
    doc = part(dot_nn(own, qu_ref[...])) + from_pieces(pieces, 0)
    gd_ref[...] = unit_grad(d_ref[...].astype(F32), inv_ref[:, 1:2], doc)


def row_columns(pair_blocks, active_pair_count, chips, core):
    slots = pair_blocks.shape[1]
    live = jnp.arange(slots)[None, :] < active_pair_count[:, None]
    rows = jnp.where(live, pair_blocks[:, :, 0], -1).reshape(1, -1)
    cols = pair_blocks[:, :, 1].reshape(1, -1)
    match = rows == (2 * jnp.arange(chips) + core)[:, None]
    low = jnp.min(jnp.where(match, cols, 2 * chips - 1), axis=1)
    high = jnp.max(jnp.where(match, cols, 0), axis=1)
    both = jnp.stack([low, high], axis=1).reshape(-1).astype(jnp.int32)
    return (both % 2 != core).astype(jnp.int32) * chips + both // 2


def on_device(query_emb, doc_emb, pair_blocks, active_pair_count):
    blocks = lax.axis_size("dp")
    chips = blocks // 2
    core = lax.axis_index("dp") % 2
    rows, features = query_emb.shape
    row_tiles, pairs = rows // SUB, features // (2 * LANES)
    assert row_tiles * pairs == chips
    groups = [[2 * chip + c for chip in range(chips)] for c in range(2)]

    def exchange(x):
        return lax.all_to_all(x, "dp", 0, 0, tiled=True, axis_index_groups=groups)

    def swap_cores(x):
        return lax.ppermute(x, "dp", [(i, i ^ 1) for i in range(blocks)])

    vmem = pltpu.VMEM
    doc_pieces = doc_emb.reshape(row_tiles, SUB, 2 * pairs, LANES).transpose(0, 2, 1, 3)
    spread = exchange(doc_pieces.reshape(chips, PIECE, LANES))
    cols = row_columns(pair_blocks, active_pair_count, chips, core)
    qu, du, inv, et_own = vmem_call(
        own_kernel,
        (vmem((rows, features), BF16), vmem((rows, features), BF16), vmem((rows, 2), F32), vmem((rows, rows), F32)),
        0,
        2,
        name="own",
    )(query_emb, doc_emb)
    wanted = vmem_call(gather_kernel, vmem((chips, 2 * PIECE, LANES), BF16), 1, 2, name="gather")(
        cols, spread, swap_cores(spread)
    )
    fetched = exchange(wanted)
    send, et, row_total, dk = vmem_call(
        tiles_kernel,
        (
            vmem((row_tiles, pairs, 4 * PIECE + SUB, LANES), BF16),
            vmem((2, rows, rows), F32),
            vmem((1, rows), F32),
            vmem((2, rows, features), BF16),
        ),
        0,
        3,
        name="tiles",
    )(qu, et_own, fetched)
    parts = exchange(send.reshape(chips, 4 * PIECE + SUB, LANES))
    to_other, acc_a, acc_b, acc_t = vmem_call(
        add_kernel,
        (
            vmem((chips, 2 * PIECE + 2 * SUB, LANES), BF16),
            vmem((blocks, PIECE, LANES), F32),
            vmem((blocks, PIECE, LANES), F32),
            vmem((blocks, SUB, LANES), F32),
        ),
        1,
        1,
        name="add",
    )(cols, parts)
    combined = vmem_call(
        finish_kernel,
        vmem((chips, PIECE + SUB, LANES), BF16),
        1,
        4,
        (pltpu.VMEM((blocks, SUB, LANES), F32),),
        name="finish",
    )(cols, swap_cores(to_other), acc_a, acc_b, acc_t)
    home = exchange(combined)
    grad = jax.ShapeDtypeStruct((rows, features), F32)
    return vmem_call(final_kernel, (grad, grad), 0, 10, name="final")(
        query_emb, doc_emb, qu, du, inv, et_own, et, row_total, dk, home
    )


def solution(mesh):
    return jax.shard_map(
        on_device,
        mesh=mesh,
        in_specs=(P("dp", None), P("dp", None), P(), P()),
        out_specs=(P("dp", None), P("dp", None)),
        check_vma=False,
    )
```

```python
import functools

import jax
import jax.numpy as jnp
from jax import lax
from jax.experimental import pallas as pl
from jax.experimental.pallas import tpu as pltpu
from jax.sharding import PartitionSpec as P

LOGIT_SCALE = 64.0
EPSILON = 1e-06
LANES = 128
SUB = 8
SHARED = 6
PLACES = 6
CHOICES = (4, 5, 6)
VMEM_BYTES = 16 * 1024 * 1024


def whole(space):
    return pl.BlockSpec(memory_space=space)


def vmem_call(body, outs, n_smem, n_vmem, scratch=(), name=None, n_any=0):
    call = pl.pallas_call(
        body,
        out_shape=outs,
        in_specs=[whole(pltpu.SMEM)] * n_smem + [whole(pl.ANY)] * n_any + [whole(pltpu.VMEM)] * n_vmem,
        out_specs=jax.tree.map(lambda _: whole(pltpu.VMEM), outs),
        scratch_shapes=list(scratch),
        compiler_params=pltpu.CompilerParams(vmem_limit_bytes=VMEM_BYTES),
        name=name,
    )

    def run(*args):
        kept = [pltpu.with_memory_space_constraint(x, pltpu.VMEM) for x in args[n_smem + n_any :]]
        return call(*args[: n_smem + n_any], *kept)

    return run


def inverse_norm(wide):
    return lax.rsqrt(jnp.sum(wide * wide, axis=1, keepdims=True) + EPSILON)


def from_pieces(pieces, slot):
    row_tiles, col_tiles = pieces.shape[:2]
    return jnp.concatenate(
        [pieces[:, ct, slot].reshape(row_tiles * SUB, LANES) for ct in range(col_tiles)], axis=1
    )


def dot_nt(a, b):
    return lax.dot_general(a, b, (((1,), (1,)), ((), ())), preferred_element_type=jnp.float32)


def dot_tn(a, b):
    return lax.dot_general(a, b, (((0,), (0,)), ((), ())), preferred_element_type=jnp.float32)


def dot_nn(a, b):
    return lax.dot_general(a, b, (((1,), (0,)), ((), ())), preferred_element_type=jnp.float32)


def own_kernel(q_ref, d_ref, qu_ref, du_ref, inv_ref, et_ref):
    q_wide = q_ref[...].astype(jnp.float32)
    d_wide = d_ref[...].astype(jnp.float32)
    q_inv = inverse_norm(q_wide)
    d_inv = inverse_norm(d_wide)
    q = (q_wide * q_inv).astype(jnp.bfloat16)
    d = (d_wide * d_inv).astype(jnp.bfloat16)
    qu_ref[...] = q
    du_ref[...] = d
    lane = lax.broadcasted_iota(jnp.int32, inv_ref.shape, 1)
    inv_ref[...] = jnp.where(lane == 0, q_inv, d_inv)
    et_ref[...] = jnp.exp(LOGIT_SCALE * dot_nt(d, q))


def split_pair(value, odd):
    high = value.astype(jnp.bfloat16).astype(jnp.float32)
    return jnp.where(odd, value - high, high)


def tiles_kernel(qu_ref, et_own_ref, fetched_ref, send_ref, et_ref, row_ref, dk_ref):
    row_tiles, col_tiles = send_ref.shape[:2]
    q = qu_ref[...]
    pieces = fetched_ref[...].astype(jnp.float32)
    pieces = pieces.reshape(row_tiles, col_tiles, 2, SUB, LANES)
    et_own = et_own_ref[...]
    row_total = jnp.sum(et_own, axis=0, keepdims=True)
    col_own = jnp.sum(et_own, axis=1, keepdims=True)
    ets, cols = [], []
    for k in range(2):
        wide = from_pieces(pieces, k)
        unit = (wide * inverse_norm(wide)).astype(jnp.bfloat16)
        dk_ref[k] = unit
        et = jnp.exp(LOGIT_SCALE * dot_nt(unit, q))
        et_ref[k] = et
        row_total = row_total + jnp.sum(et, axis=0, keepdims=True)
        cols.append(jnp.sum(et, axis=1, keepdims=True))
        ets.append(et)
    row_ref[...] = row_total
    row_inv = 1.0 / row_total
    half = 0.5 * LOGIT_SCALE
    parts = []
    for make in (lambda e: e * row_inv, lambda e: e):
        parts.append([half * dot_nn(make(e).astype(jnp.bfloat16), q) for e in ets])
    for ct in range(col_tiles):
        lanes = slice(ct * LANES, (ct + 1) * LANES)
        for kind in range(2):
            pair = [x[:, lanes].reshape(row_tiles, 1, SUB, LANES) for x in parts[kind]]
            both = jnp.concatenate(pair, axis=1).reshape(row_tiles, 2 * SUB, LANES)
            send_ref[:, ct, 2 * SUB * kind : 2 * SUB * (kind + 1), :] = both.astype(jnp.bfloat16)
    rows = row_tiles * SUB
    lane = lax.broadcasted_iota(jnp.int32, (rows, LANES), 1)
    value = jnp.where(lane < 2, col_own, jnp.where(lane < 4, cols[0], cols[1]))
    scalars = split_pair(value, lane % 2 == 1).reshape(row_tiles, SUB, LANES).astype(jnp.bfloat16)
    for ct in range(col_tiles):
        send_ref[:, ct, 4 * SUB :, :] = scalars


def combine_kernel(cols_ref, recv_ref, out_ref, acc_a, acc_b, acc_t):
    blocks = recv_ref.shape[0]
    acc_a[...] = jnp.zeros_like(acc_a)
    acc_b[...] = jnp.zeros_like(acc_b)
    lane3 = lax.broadcasted_iota(jnp.int32, acc_t.shape, 2)
    own = recv_ref[:, 4 * SUB :, :].astype(jnp.float32)
    acc_t[...] = jnp.where(lane3 < 2, own, 0.0)
    lane = lax.broadcasted_iota(jnp.int32, (SUB, LANES), 1)
    masks = [(lane >= 2) & (lane < 4), (lane >= 4) & (lane < 6)]

    def add(source, carry):
        a = recv_ref[source, 0 : 2 * SUB, :].astype(jnp.float32)
        b = recv_ref[source, 2 * SUB : 4 * SUB, :].astype(jnp.float32)
        t = recv_ref[source, 4 * SUB :, :].astype(jnp.float32)
        for k in range(2):
            col = cols_ref[2 * source + k]
            acc_a[col] = acc_a[col] + a[k * SUB : (k + 1) * SUB]
            acc_b[col] = acc_b[col] + b[k * SUB : (k + 1) * SUB]
            acc_t[col] = acc_t[col] + jnp.where(masks[k], t, 0.0)
        return carry

    lax.fori_loop(0, blocks, add, 0, unroll=8)
    total = jnp.broadcast_to(jnp.sum(acc_t[...], axis=2, keepdims=True), acc_t.shape)
    acc_t[...] = total
    acc_a[...] = acc_a[...] + acc_b[...] / total
    odd = lane % 2 == 1

    def emit(dest, carry):
        value = jnp.where(
            lane < 2,
            acc_t[dest],
            jnp.where(lane < 4, acc_t[cols_ref[2 * dest]], acc_t[cols_ref[2 * dest + 1]]),
        )
        both = jnp.concatenate([acc_a[dest], split_pair(value, odd)], axis=0)
        out_ref[dest] = both.astype(jnp.bfloat16)
        return carry

    lax.fori_loop(0, blocks, emit, 0, unroll=8)


def unit_grad(wide, inverse, upstream):
    radial = jnp.sum(wide * upstream, axis=1, keepdims=True)
    return upstream * inverse - wide * (radial * inverse * inverse * inverse)


def final_kernel(
    q_ref, d_ref, qu_ref, du_ref, inv_ref, et_own_ref, et_ref, row_ref, dk_ref, home_ref, gq_ref, gd_ref
):
    rows, features = q_ref.shape
    row_tiles, col_tiles = rows // SUB, features // LANES
    pieces = home_ref[...].astype(jnp.float32).reshape(row_tiles, col_tiles, 2, SUB, LANES)
    scalars = pieces[:, 0, 1].reshape(rows, LANES)
    totals = [scalars[:, 2 * i : 2 * i + 1] + scalars[:, 2 * i + 1 : 2 * i + 2] for i in range(3)]
    row_inv = 1.0 / row_ref[...]

    def weight(et, total):
        return 0.5 * (et * row_inv + et * (1.0 / total))

    own = weight(et_own_ref[...], totals[0])
    diagonal = lax.broadcasted_iota(jnp.int32, own.shape, 0) == lax.broadcasted_iota(
        jnp.int32, own.shape, 1
    )
    own = (own - jnp.where(diagonal, 1.0, 0.0)).astype(jnp.bfloat16)

    def part(x):
        return (LOGIT_SCALE * x).astype(jnp.bfloat16).astype(jnp.float32)

    query = part(dot_tn(own, du_ref[...]))
    for k in range(2):
        w = weight(et_ref[k], totals[k + 1]).astype(jnp.bfloat16)
        query = query + part(dot_tn(w, dk_ref[k]))
    gq_ref[...] = unit_grad(q_ref[...].astype(jnp.float32), inv_ref[:, 0:1], query)
    doc = part(dot_nn(own, qu_ref[...])) + from_pieces(pieces, 0)
    gd_ref[...] = unit_grad(d_ref[...].astype(jnp.float32), inv_ref[:, 1:2], doc)


def gather_many_kernel(table_ref, spread_ref, out_ref):
    slots = out_ref.shape[1] // SUB
    stride = table_ref.shape[0] // out_ref.shape[0]

    def step(dest, carry):
        tiles = []
        for slot in range(slots):
            at = table_ref[dest * stride + slot]
            tiles.append(spread_ref[at])
        for slot in range(slots):
            out_ref[dest, slot * SUB : (slot + 1) * SUB, :] = tiles[slot]
        return carry

    lax.fori_loop(0, out_ref.shape[0], step, 0, unroll=4)


def pack_kernel(q_ref, d_ref, out_ref, q_buf, d_buf, out_buf, in_sems, out_sems):
    parts = in_sems.shape[1]
    step = q_ref.shape[0] // parts
    reads, writes = [], []
    for j in range(parts):
        some = pl.ds(j * step, step)
        reads.append(
            [
                pltpu.make_async_copy(ref.at[some], buf.at[some], in_sems.at[i, j])
                for i, (ref, buf) in enumerate(((q_ref, q_buf), (d_ref, d_buf)))
            ]
        )
        writes.append(pltpu.make_async_copy(out_buf.at[some], out_ref.at[some], out_sems.at[j]))
    for pair in reads:
        for copy in pair:
            copy.start()
    for j in range(parts):
        for copy in reads[j]:
            copy.wait()
        some = slice(j * step, (j + 1) * step)
        out_buf[some, 0:SUB, :] = q_buf[some]
        out_buf[some, SUB:, :] = d_buf[some]
        writes[j].start()
    for copy in writes:
        copy.wait()


def pack(q, d):
    blocks = q.shape[0]
    anywhere = pl.BlockSpec(memory_space=pl.ANY)
    parts = 2
    return pl.pallas_call(
        pack_kernel,
        out_shape=jax.ShapeDtypeStruct((blocks, 2 * SUB, LANES), q.dtype),
        in_specs=[anywhere, anywhere],
        out_specs=anywhere,
        scratch_shapes=[
            pltpu.VMEM(q.shape, q.dtype),
            pltpu.VMEM(d.shape, d.dtype),
            pltpu.VMEM((blocks, 2 * SUB, LANES), q.dtype),
            pltpu.SemaphoreType.DMA((2, parts)),
            pltpu.SemaphoreType.DMA((parts,)),
        ],
        compiler_params=pltpu.CompilerParams(vmem_limit_bytes=VMEM_BYTES),
        name="pack",
    )(q, d)


def eye_mask(n):
    return lax.broadcasted_iota(jnp.int32, (n, n), 0) == lax.broadcasted_iota(jnp.int32, (n, n), 1)


def to_lanes(column, eye):
    return jnp.sum(jnp.where(eye, column, 0.0), axis=0, keepdims=True)


def to_sublanes(row, eye):
    return jnp.sum(jnp.where(eye, row, 0.0), axis=1, keepdims=True)


def own_pair_kernel(q_ref, d_ref, qu_ref, du_ref, inv_ref, e_ref, et_ref):
    own_kernel(q_ref, d_ref, qu_ref, du_ref, inv_ref, et_ref)
    e_ref[...] = jnp.exp(LOGIT_SCALE * dot_nt(qu_ref[...], du_ref[...]))


def both_tiles_kernel(
    info_ref, other_any, qu_ref, du_ref, e_own_ref, et_own_ref, fetched_ref,
    send_ref, e_ref, et_ref, row_ref, dk_ref, qs_ref, other_ref, sem
):
    bring = pltpu.make_async_copy(other_any, other_ref, sem)
    bring.start()
    rows, features = qu_ref.shape
    row_tiles, col_tiles = rows // SUB, features // LANES
    eye = eye_mask(rows)

    def fetched(slot):
        piece = fetched_ref[:, slot * SUB : (slot + 1) * SUB, :].astype(jnp.float32)
        piece = piece.reshape(row_tiles, col_tiles, 1, SUB, LANES)
        wide = from_pieces(piece, 0)
        return (wide * inverse_norm(wide)).astype(jnp.bfloat16)

    q = qu_ref[...]
    row_total = jnp.sum(e_own_ref[...], axis=1, keepdims=True)
    for k in range(2):
        unit = fetched(k)
        dk_ref[k] = unit
        e = jnp.exp(LOGIT_SCALE * dot_nt(q, unit))
        e_ref[k] = e
        row_total = row_total + jnp.sum(e, axis=1, keepdims=True)
    row_ref[...] = row_total
    sums = [jnp.sum(et_own_ref[...], axis=1, keepdims=True), jnp.zeros((rows, 1), jnp.float32)]
    bring.wait()
    for slot in range(qs_ref.shape[0]):
        entry = info_ref[PLACES + slot]
        live = entry > 0
        partner = lax.rem(entry, 2) == 0
        unit = fetched(slot + 2)
        qs_ref[slot] = unit
        docs = jnp.where(partner, other_ref[...], du_ref[...])
        et = jnp.exp(LOGIT_SCALE * dot_nt(docs, unit))
        et = jnp.where(live, et, 0.0)
        et_ref[slot] = et
        total = jnp.sum(et, axis=1, keepdims=True)
        sums[0] = sums[0] + jnp.where(partner, 0.0, total)
        sums[1] = sums[1] + jnp.where(partner, total, 0.0)
    message = jnp.concatenate([to_lanes(x, eye) for x in (row_total, *sums)], axis=1)
    send_ref[...] = jnp.broadcast_to(message[None], send_ref.shape)


def sums_of(table_ref, block, which):
    return table_ref[block, :, which * LANES : (which + 1) * LANES]


def doc_side_kernel(
    info_ref, table_ref, qu_ref, et_own_ref, et_ref, qs_ref, acc_ref, other_ref, both_ref
):
    rows = et_own_ref.shape[0]
    eye = eye_mask(rows)
    me = info_ref[0]
    pal = info_ref[1]
    mine_total = sums_of(table_ref, me, 1) + sums_of(table_ref, pal, 2)
    pal_total = sums_of(table_ref, pal, 1) + sums_of(table_ref, me, 2)
    inverse = [1.0 / to_sublanes(mine_total, eye), 1.0 / to_sublanes(pal_total, eye)]

    def part(x):
        return (LOGIT_SCALE * x).astype(jnp.bfloat16).astype(jnp.float32)

    def weight(et, row_total, col_inverse):
        return 0.5 * (et * (1.0 / row_total) + et * col_inverse)

    own = weight(et_own_ref[...], sums_of(table_ref, me, 0), inverse[0])
    own = (own - jnp.where(eye, 1.0, 0.0)).astype(jnp.bfloat16)
    both_ref[0] = part(dot_nn(own, qu_ref[...]))
    both_ref[1] = jnp.zeros(both_ref.shape[1:], jnp.float32)
    for slot in range(qs_ref.shape[0]):
        entry = info_ref[PLACES + slot]

        @pl.when(entry > 0)
        def _():
            side = 1 - lax.rem(entry, 2)
            block = (entry - 1) // 2
            w = weight(et_ref[slot], sums_of(table_ref, block, 0), jnp.where(side == 1, inverse[1], inverse[0]))
            both_ref[side] = both_ref[side] + part(dot_nn(w.astype(jnp.bfloat16), qs_ref[slot]))

    acc_ref[...] = both_ref[0]
    other_ref[...] = both_ref[1].astype(jnp.bfloat16)


def query_side_kernel(
    info_ref, table_ref, q_ref, du_ref, inv_ref, e_own_ref, e_ref, row_ref, dk_ref, gq_ref
):
    eye = eye_mask(q_ref.shape[0])
    row_inv = 1.0 / row_ref[...]

    def total(col, pal):
        return sums_of(table_ref, col, 1) + sums_of(table_ref, pal, 2)

    def weight(e, col_total):
        return 0.5 * (e * row_inv + e * (1.0 / col_total))

    def part(x):
        return (LOGIT_SCALE * x).astype(jnp.bfloat16).astype(jnp.float32)

    own = weight(e_own_ref[...], total(info_ref[0], info_ref[1]))
    query = part(dot_nn((own - jnp.where(eye, 1.0, 0.0)).astype(jnp.bfloat16), du_ref[...]))
    for k in range(2):
        w = weight(e_ref[k], total(info_ref[2 + 2 * k], info_ref[3 + 2 * k]))
        query = query + part(dot_nn(w.astype(jnp.bfloat16), dk_ref[k]))
    gq_ref[...] = unit_grad(q_ref[...].astype(jnp.float32), inv_ref[:, 0:1], query)


def doc_final_kernel(d_ref, inv_ref, acc_ref, swapped_ref, gd_ref):
    doc = acc_ref[...] + swapped_ref[...].astype(jnp.float32)
    gd_ref[...] = unit_grad(d_ref[...].astype(jnp.float32), inv_ref[:, 1:2], doc)


def exchange(x):
    return lax.all_to_all(x, "dp", split_axis=0, concat_axis=0, tiled=True)


def row_columns(pair_blocks, active_pair_count, blocks):
    slots = pair_blocks.shape[1]
    live = jnp.arange(slots)[None, :] < active_pair_count[:, None]
    rows = jnp.where(live, pair_blocks[:, :, 0], -1).reshape(1, -1)
    cols = pair_blocks[:, :, 1].reshape(1, -1)
    match = rows == jnp.arange(blocks)[:, None]
    low = jnp.min(jnp.where(match, cols, blocks - 1), axis=1)
    high = jnp.max(jnp.where(match, cols, 0), axis=1)
    return jnp.stack([low, high], axis=1).reshape(-1).astype(jnp.int32)


def shared_slots(cols, blocks):
    tiles = jnp.arange(cols.shape[0])
    chip = cols // 2
    before = (chip[:, None] == chip[None, :]) & (tiles[None, :] < tiles[:, None])
    rank = jnp.sum(before.astype(jnp.int32), axis=1)
    device = 2 * chip + rank % 2
    slot = rank // 2
    entry = 1 + 2 * (tiles // 2) + (cols % 2 != rank % 2).astype(jnp.int32)
    place = device * SHARED + slot
    hit = (place[None, :] == jnp.arange(blocks * SHARED)[:, None]) & (slot[None, :] < SHARED)
    table = jnp.sum(jnp.where(hit, entry[None, :], 0), axis=1).astype(jnp.int32)
    return table.reshape(blocks, SHARED), jnp.max(rank)


def general_path(query_emb, doc_emb, spread, cols, wanted_tiles, info):
    blocks = lax.axis_size("dp")
    rows, features = query_emb.shape
    row_tiles, col_tiles = rows // SUB, features // LANES
    sds = pltpu.VMEM
    bf16, f32 = jnp.bfloat16, jnp.float32
    qu, du, inv, et_own = vmem_call(
        own_kernel,
        (sds((rows, features), bf16), sds((rows, features), bf16), sds((rows, 2), f32), sds((rows, rows), f32)),
        0,
        2,
        name="own",
    )(query_emb, doc_emb)
    wanted = vmem_call(gather_many_kernel, sds((blocks, 2 * SUB, LANES), bf16), 1, 1, name="gather")(
        wanted_tiles, spread.reshape(2 * blocks, SUB, LANES)
    )
    fetched = exchange(wanted)
    send, et, row_total, dk = vmem_call(
        tiles_kernel,
        (
            sds((row_tiles, col_tiles, 5 * SUB, LANES), bf16),
            sds((2, rows, rows), f32),
            sds((1, rows), f32),
            sds((2, rows, features), bf16),
        ),
        0,
        3,
        name="tiles",
    )(qu, et_own, fetched)
    parts = exchange(send.reshape(blocks, 5 * SUB, LANES))
    acc = pltpu.VMEM((blocks, SUB, LANES), f32)
    combined = vmem_call(
        combine_kernel, sds((blocks, 2 * SUB, LANES), bf16), 1, 1, (acc, acc, acc), name="combine"
    )(cols, parts)
    home = exchange(combined)
    grad = jax.ShapeDtypeStruct((rows, features), f32)
    return vmem_call(final_kernel, (grad, grad), 0, 10, name="final")(
        query_emb, doc_emb, qu, du, inv, et_own, et, row_total, dk, home
    )


def short_path(shared, query_emb, doc_emb, spread, cols, wanted_tiles, info):
    blocks = lax.axis_size("dp")
    rows, features = query_emb.shape
    assert rows == LANES
    sds = pltpu.VMEM
    bf16, f32 = jnp.bfloat16, jnp.float32
    mat, wide = sds((rows, rows), f32), sds((rows, features), bf16)
    grad = jax.ShapeDtypeStruct((rows, features), f32)
    slots = 2 + shared
    wanted = vmem_call(gather_many_kernel, sds((blocks, slots * SUB, LANES), bf16), 1, 1, name="gather")(
        wanted_tiles, spread.reshape(2 * blocks, SUB, LANES)
    )
    fetched = exchange(wanted)
    qu, du, inv, e_own, et_own = vmem_call(
        own_pair_kernel, (wide, wide, sds((rows, 2), f32), mat, mat), 0, 2, name="own"
    )(query_emb, doc_emb)
    send, e, et, row_total, dk, qs = vmem_call(
        both_tiles_kernel,
        (
            sds((blocks, 1, 3 * rows), f32),
            sds((2, rows, rows), f32),
            sds((shared, rows, rows), f32),
            sds((rows, 1), f32),
            sds((2, rows, features), bf16),
            sds((shared, rows, features), bf16),
        ),
        1,
        5,
        (pltpu.VMEM((rows, features), bf16), pltpu.SemaphoreType.DMA),
        name="tiles",
        n_any=1,
    )(info, swap_cores(du), qu, du, e_own, et_own, fetched)
    totals = exchange(send)
    acc, to_other = vmem_call(
        doc_side_kernel,
        (sds((rows, features), f32), wide),
        1,
        5,
        (pltpu.VMEM((2, rows, features), f32),),
        name="docs",
    )(info, totals, qu, et_own, et, qs)
    swapped = swap_cores(to_other)
    grad_query = vmem_call(query_side_kernel, grad, 1, 8, name="queries")(
        info, totals, query_emb, du, inv, e_own, e, row_total, dk
    )
    grad_doc = vmem_call(doc_final_kernel, grad, 0, 4, name="final")(doc_emb, inv, acc, swapped)
    return grad_query, grad_doc


def swap_cores(x):
    return lax.ppermute(x, "dp", [(i, i ^ 1) for i in range(lax.axis_size("dp"))])


def on_device(query_emb, doc_emb, pair_blocks, active_pair_count):
    blocks = lax.axis_size("dp")
    me = lax.axis_index("dp")
    rows, features = query_emb.shape
    row_tiles, col_tiles = rows // SUB, features // LANES
    assert row_tiles * col_tiles == blocks

    def pieces(x):
        tiled = x.reshape(row_tiles, SUB, col_tiles, LANES).transpose(0, 2, 1, 3)
        return tiled.reshape(blocks, SUB, LANES)

    spread = exchange(pack(pieces(query_emb), pieces(doc_emb)))
    cols = row_columns(pair_blocks, active_pair_count, blocks)
    table, deepest = shared_slots(cols, blocks)
    wanted_tiles = jnp.concatenate(
        [2 * cols.reshape(blocks, 2) + 1, 2 * (jnp.maximum(table - 1, 0) // 2)], axis=1
    ).reshape(-1)
    low, high = jnp.split(lax.dynamic_slice_in_dim(cols, 2 * me, 2), 2)
    self_id = me.reshape(1).astype(jnp.int32)
    mine = lax.dynamic_index_in_dim(table, me, 0, keepdims=False)
    info = jnp.concatenate([self_id, self_id ^ 1, low, low ^ 1, high, high ^ 1, mine])
    choice = sum((deepest >= 2 * shared).astype(jnp.int32) for shared in CHOICES)
    cols, wanted_tiles, info, choice = lax.optimization_barrier((cols, wanted_tiles, info, choice))
    args = (query_emb, doc_emb, spread, cols, wanted_tiles, info)
    paths = [functools.partial(short_path, shared) for shared in CHOICES] + [general_path]
    return lax.switch(choice, paths, *args)


def solution(mesh):
    return jax.shard_map(
        on_device,
        mesh=mesh,
        in_specs=(P("dp", None), P("dp", None), P(), P()),
        out_specs=(P("dp", None), P("dp", None)),
        check_vma=False,
    )
```

```python
import functools

import jax
import jax.numpy as jnp
from jax import lax
from jax.experimental import pallas as pl
from jax.experimental.pallas import tpu as pltpu
from jax.sharding import PartitionSpec as P

LOGIT_SCALE = 64.0
EPSILON = 1e-06
LANES = 128
SUB = 8
SHARED = 6
PICKS = 16
CHOICES = (4, 5, 6)
VMEM_BYTES = 16 * 1024 * 1024


def whole(space):
    return pl.BlockSpec(memory_space=space)


def vmem_call(body, outs, n_smem, n_vmem, scratch=(), name=None, n_any=0, out_space=pltpu.VMEM, keep=True):
    call = pl.pallas_call(
        body,
        out_shape=outs,
        in_specs=[whole(pltpu.SMEM)] * n_smem + [whole(pl.ANY)] * n_any + [whole(pltpu.VMEM)] * n_vmem,
        out_specs=jax.tree.map(lambda _: whole(out_space), outs),
        scratch_shapes=list(scratch),
        compiler_params=pltpu.CompilerParams(vmem_limit_bytes=VMEM_BYTES),
        name=name,
    )

    def run(*args):
        if not keep:
            return call(*args)
        kept = [pltpu.with_memory_space_constraint(x, pltpu.VMEM) for x in args[n_smem + n_any :]]
        return call(*args[: n_smem + n_any], *kept)

    return run


def inverse_norm(wide):
    return lax.rsqrt(jnp.sum(wide * wide, axis=1, keepdims=True) + EPSILON)


def from_pieces(pieces, slot):
    row_tiles, col_tiles = pieces.shape[:2]
    return jnp.concatenate(
        [pieces[:, ct, slot].reshape(row_tiles * SUB, LANES) for ct in range(col_tiles)], axis=1
    )


def dot_nt(a, b):
    return lax.dot_general(a, b, (((1,), (1,)), ((), ())), preferred_element_type=jnp.float32)


def dot_tn(a, b):
    return lax.dot_general(a, b, (((0,), (0,)), ((), ())), preferred_element_type=jnp.float32)


def dot_nn(a, b):
    return lax.dot_general(a, b, (((1,), (0,)), ((), ())), preferred_element_type=jnp.float32)


def own_kernel(q_ref, d_ref, qu_ref, du_ref, inv_ref, et_ref):
    q_wide = q_ref[...].astype(jnp.float32)
    d_wide = d_ref[...].astype(jnp.float32)
    q_inv = inverse_norm(q_wide)
    d_inv = inverse_norm(d_wide)
    q = (q_wide * q_inv).astype(jnp.bfloat16)
    d = (d_wide * d_inv).astype(jnp.bfloat16)
    qu_ref[...] = q
    du_ref[...] = d
    lane = lax.broadcasted_iota(jnp.int32, inv_ref.shape, 1)
    inv_ref[...] = jnp.where(lane == 0, q_inv, d_inv)
    et_ref[...] = jnp.exp(LOGIT_SCALE * dot_nt(d, q))


def split_pair(value, odd):
    high = value.astype(jnp.bfloat16).astype(jnp.float32)
    return jnp.where(odd, value - high, high)


def tiles_kernel(qu_ref, et_own_ref, fetched_ref, send_ref, et_ref, row_ref, dk_ref):
    row_tiles, col_tiles = send_ref.shape[:2]
    q = qu_ref[...]
    pieces = fetched_ref[:, 0 : 2 * SUB, :].astype(jnp.float32)
    pieces = pieces.reshape(row_tiles, col_tiles, 2, SUB, LANES)
    et_own = et_own_ref[...]
    row_total = jnp.sum(et_own, axis=0, keepdims=True)
    col_own = jnp.sum(et_own, axis=1, keepdims=True)
    ets, cols = [], []
    for k in range(2):
        wide = from_pieces(pieces, k)
        unit = (wide * inverse_norm(wide)).astype(jnp.bfloat16)
        dk_ref[k] = unit
        et = jnp.exp(LOGIT_SCALE * dot_nt(unit, q))
        et_ref[k] = et
        row_total = row_total + jnp.sum(et, axis=0, keepdims=True)
        cols.append(jnp.sum(et, axis=1, keepdims=True))
        ets.append(et)
    row_ref[...] = row_total
    row_inv = 1.0 / row_total
    half = 0.5 * LOGIT_SCALE
    parts = []
    for make in (lambda e: e * row_inv, lambda e: e):
        parts.append([half * dot_nn(make(e).astype(jnp.bfloat16), q) for e in ets])
    for ct in range(col_tiles):
        lanes = slice(ct * LANES, (ct + 1) * LANES)
        for kind in range(2):
            pair = [x[:, lanes].reshape(row_tiles, 1, SUB, LANES) for x in parts[kind]]
            both = jnp.concatenate(pair, axis=1).reshape(row_tiles, 2 * SUB, LANES)
            send_ref[:, ct, 2 * SUB * kind : 2 * SUB * (kind + 1), :] = both.astype(jnp.bfloat16)
    rows = row_tiles * SUB
    lane = lax.broadcasted_iota(jnp.int32, (rows, LANES), 1)
    value = jnp.where(lane < 2, col_own, jnp.where(lane < 4, cols[0], cols[1]))
    scalars = split_pair(value, lane % 2 == 1).reshape(row_tiles, SUB, LANES).astype(jnp.bfloat16)
    for ct in range(col_tiles):
        send_ref[:, ct, 4 * SUB :, :] = scalars


def combine_kernel(cols_ref, recv_ref, out_ref, acc_a, acc_b, acc_t):
    blocks = recv_ref.shape[0]
    acc_a[...] = jnp.zeros_like(acc_a)
    acc_b[...] = jnp.zeros_like(acc_b)
    lane3 = lax.broadcasted_iota(jnp.int32, acc_t.shape, 2)
    own = recv_ref[:, 4 * SUB :, :].astype(jnp.float32)
    acc_t[...] = jnp.where(lane3 < 2, own, 0.0)
    lane = lax.broadcasted_iota(jnp.int32, (SUB, LANES), 1)
    masks = [(lane >= 2) & (lane < 4), (lane >= 4) & (lane < 6)]

    def add(source, carry):
        a = recv_ref[source, 0 : 2 * SUB, :].astype(jnp.float32)
        b = recv_ref[source, 2 * SUB : 4 * SUB, :].astype(jnp.float32)
        t = recv_ref[source, 4 * SUB :, :].astype(jnp.float32)
        for k in range(2):
            col = cols_ref[2 * source + k]
            acc_a[col] = acc_a[col] + a[k * SUB : (k + 1) * SUB]
            acc_b[col] = acc_b[col] + b[k * SUB : (k + 1) * SUB]
            acc_t[col] = acc_t[col] + jnp.where(masks[k], t, 0.0)
        return carry

    lax.fori_loop(0, blocks, add, 0, unroll=8)
    total = jnp.broadcast_to(jnp.sum(acc_t[...], axis=2, keepdims=True), acc_t.shape)
    acc_t[...] = total
    acc_a[...] = acc_a[...] + acc_b[...] / total
    odd = lane % 2 == 1

    def emit(dest, carry):
        value = jnp.where(
            lane < 2,
            acc_t[dest],
            jnp.where(lane < 4, acc_t[cols_ref[2 * dest]], acc_t[cols_ref[2 * dest + 1]]),
        )
        both = jnp.concatenate([acc_a[dest], split_pair(value, odd)], axis=0)
        out_ref[dest] = both.astype(jnp.bfloat16)
        return carry

    lax.fori_loop(0, blocks, emit, 0, unroll=8)


def unit_grad(wide, inverse, upstream):
    radial = jnp.sum(wide * upstream, axis=1, keepdims=True)
    return upstream * inverse - wide * (radial * inverse * inverse * inverse)


def final_kernel(
    q_ref, d_ref, qu_ref, du_ref, inv_ref, et_own_ref, et_ref, row_ref, dk_ref, home_ref, gq_ref, gd_ref
):
    rows, features = q_ref.shape
    row_tiles, col_tiles = rows // SUB, features // LANES
    pieces = home_ref[...].astype(jnp.float32).reshape(row_tiles, col_tiles, 2, SUB, LANES)
    scalars = pieces[:, 0, 1].reshape(rows, LANES)
    totals = [scalars[:, 2 * i : 2 * i + 1] + scalars[:, 2 * i + 1 : 2 * i + 2] for i in range(3)]
    row_inv = 1.0 / row_ref[...]

    def weight(et, total):
        return 0.5 * (et * row_inv + et * (1.0 / total))

    own = weight(et_own_ref[...], totals[0])
    diagonal = lax.broadcasted_iota(jnp.int32, own.shape, 0) == lax.broadcasted_iota(
        jnp.int32, own.shape, 1
    )
    own = (own - jnp.where(diagonal, 1.0, 0.0)).astype(jnp.bfloat16)

    def part(x):
        return (LOGIT_SCALE * x).astype(jnp.bfloat16).astype(jnp.float32)

    query = part(dot_tn(own, du_ref[...]))
    for k in range(2):
        w = weight(et_ref[k], totals[k + 1]).astype(jnp.bfloat16)
        query = query + part(dot_tn(w, dk_ref[k]))
    gq_ref[...] = unit_grad(q_ref[...].astype(jnp.float32), inv_ref[:, 0:1], query)
    doc = part(dot_nn(own, qu_ref[...])) + from_pieces(pieces, 0)
    gd_ref[...] = unit_grad(d_ref[...].astype(jnp.float32), inv_ref[:, 1:2], doc)


def first_gather_kernel(cols_ref, spread_ref, query_ref, out_ref):
    def step(dest, carry):
        tiles = [spread_ref[cols_ref[2 * dest + k]] for k in range(2)] + [query_ref[dest]]
        for slot, tile in enumerate(tiles):
            out_ref[dest, slot * SUB : (slot + 1) * SUB, :] = tile
        return carry

    lax.fori_loop(0, out_ref.shape[0], step, 0, unroll=8)


def eye_mask(n):
    return lax.broadcasted_iota(jnp.int32, (n, n), 0) == lax.broadcasted_iota(jnp.int32, (n, n), 1)


def to_lanes(column, eye):
    return jnp.sum(jnp.where(eye, column, 0.0), axis=0, keepdims=True)


def to_sublanes(row, eye):
    return jnp.sum(jnp.where(eye, row, 0.0), axis=1, keepdims=True)


def own_pair_kernel(q_ref, d_ref, qu_ref, du_ref, inv_ref, e_ref, et_ref):
    own_kernel(q_ref, d_ref, qu_ref, du_ref, inv_ref, et_ref)
    e_ref[...] = jnp.exp(LOGIT_SCALE * dot_nt(qu_ref[...], du_ref[...]))


def fetched_rows(fetched_ref, slot, row_tiles, col_tiles):
    piece = fetched_ref[:, slot * SUB : (slot + 1) * SUB, :].astype(jnp.float32)
    return from_pieces(piece.reshape(row_tiles, col_tiles, 1, SUB, LANES), 0)


def row_side_kernel(
    table_ref, qu_ref, du_ref, e_own_ref, et_own_ref, fetched_ref, send_ref, e_ref, row_ref, units_ref, extra_ref
):
    rows, features = qu_ref.shape
    row_tiles, col_tiles = rows // SUB, features // LANES
    shared = send_ref.shape[1] // SUB - 1
    stride = table_ref.shape[0] // send_ref.shape[0]
    eye = eye_mask(rows)
    q = qu_ref[...]
    units_ref[0:rows] = du_ref[...]
    row_total = jnp.sum(e_own_ref[...], axis=1, keepdims=True)
    columns = [to_lanes(jnp.sum(et_own_ref[...], axis=1, keepdims=True), eye)]
    for k in range(2):
        wide = fetched_rows(fetched_ref, k, row_tiles, col_tiles)
        unit = (wide * inverse_norm(wide)).astype(jnp.bfloat16)
        units_ref[(k + 1) * rows : (k + 2) * rows] = unit
        e = jnp.exp(LOGIT_SCALE * dot_nt(q, unit))
        e_ref[k] = e
        row_total = row_total + jnp.sum(e, axis=1, keepdims=True)
        columns.append(jnp.sum(e, axis=0, keepdims=True))
    row_ref[...] = row_total
    doubled = []
    for x in [to_lanes(row_total, eye)] + columns:
        high = x.astype(jnp.bfloat16).astype(jnp.float32)
        doubled += [high, x - high]
    extra_ref[...] = jnp.concatenate(doubled, axis=0).astype(jnp.bfloat16)
    send_ref[:, shared * SUB :, :] = jnp.broadcast_to(extra_ref[...][None], (send_ref.shape[0], SUB, LANES))

    def step(dest, carry):
        tiles = [
            fetched_ref[table_ref[dest * stride + slot], 2 * SUB : 3 * SUB, :] for slot in range(shared)
        ]
        for slot, tile in enumerate(tiles):
            send_ref[dest, slot * SUB : (slot + 1) * SUB, :] = tile
        return carry

    lax.fori_loop(0, send_ref.shape[0], step, 0, unroll=4)


def doc_side_kernel(
    info_ref, other_any, pick_ref, qu_ref, du_ref, et_own_ref, recv_ref,
    acc_ref, partner_ref, sums_ref, units_ref, other_ref, sem
):
    bring = pltpu.make_async_copy(other_any, other_ref, sem)
    bring.start()
    rows, features = qu_ref.shape
    row_tiles, col_tiles = rows // SUB, features // LANES
    blocks = recv_ref.shape[0]
    shared = recv_ref.shape[1] // SUB - 1
    eye = eye_mask(rows)
    messages = recv_ref[:, shared * SUB :, :].astype(jnp.float32).reshape(blocks * SUB, LANES)
    sums = dot_nn(pick_ref[...], messages.astype(jnp.bfloat16))
    sums_ref[...] = sums
    inverse = [1.0 / to_sublanes(sums[i : i + 1], eye) for i in range(2)]

    def weight(et, row_total, col_inverse):
        return 0.5 * (et * (1.0 / row_total) + et * col_inverse)

    q = qu_ref[...]
    own = weight(et_own_ref[...], sums[4:5], inverse[0]) - jnp.where(eye, 1.0, 0.0)
    units_ref[0:rows] = q
    weights = [[own.astype(jnp.bfloat16)], [jnp.zeros((rows, rows), jnp.bfloat16)]]
    bring.wait()
    for slot in range(shared):
        entry = info_ref[slot]
        side = 1 - lax.rem(entry, 2)
        unit = fetched_rows(recv_ref, slot, row_tiles, col_tiles).astype(jnp.bfloat16)
        units_ref[(slot + 1) * rows : (slot + 2) * rows] = unit
        docs = jnp.where(side == 1, other_ref[...], du_ref[...])
        et = jnp.exp(LOGIT_SCALE * dot_nt(docs, unit))
        live = entry > 0
        total = jnp.where(live, sums[5 + slot : 6 + slot], 1.0)
        w = weight(et, total, jnp.where(side == 1, inverse[1], inverse[0]))
        for i in range(2):
            weights[i].append(jnp.where(live & (side == i), w, 0.0).astype(jnp.bfloat16))
    weights = jnp.concatenate([jnp.concatenate(w, axis=1) for w in weights], axis=0)
    grads = LOGIT_SCALE * dot_nn(weights, units_ref[...])
    acc_ref[...] = grads[0:rows]
    partner_ref[...] = grads[rows:].astype(jnp.bfloat16)


def query_side_kernel(sums_ref, q_ref, inv_ref, e_own_ref, e_ref, row_ref, units_ref, gq_ref, buf, sems):
    eye = eye_mask(q_ref.shape[0])
    row_inv = 1.0 / row_ref[...]

    def weight(e, which):
        return 0.5 * (e * row_inv + e * (1.0 / sums_ref[which : which + 1, :]))

    weights = [weight(e_own_ref[...], 0) - jnp.where(eye, 1.0, 0.0)]
    weights += [weight(e_ref[k], 2 + k) for k in range(2)]
    query = LOGIT_SCALE * dot_nn(jnp.concatenate(weights, axis=1).astype(jnp.bfloat16), units_ref[...])
    write_grad(gq_ref, buf, sems, lambda some: (q_ref[some], inv_ref[some, 0:1], query[some]))


def write_grad(out_ref, buf, sems, rows_of):
    parts = sems.shape[0]
    step = buf.shape[0] // parts
    copies = []
    for j in range(parts):
        some = slice(j * step, (j + 1) * step)
        raw, inverse, upstream = rows_of(some)
        buf[some] = unit_grad(raw.astype(jnp.float32), inverse, upstream)
        at = pl.ds(j * step, step)
        copies.append(pltpu.make_async_copy(buf.at[at], out_ref.at[at], sems.at[j]))
        copies[-1].start()
    for copy in copies:
        copy.wait()


def doc_final_kernel(d_ref, inv_ref, acc_ref, swapped_ref, gd_ref, buf, sems):
    def rows_of(some):
        return d_ref[some], inv_ref[some, 1:2], acc_ref[some] + swapped_ref[some].astype(jnp.float32)

    write_grad(gd_ref, buf, sems, rows_of)


def exchange(x):
    return lax.all_to_all(x, "dp", split_axis=0, concat_axis=0, tiled=True)


def row_columns(pair_blocks, active_pair_count, blocks):
    slots = pair_blocks.shape[1]
    live = jnp.arange(slots)[None, :] < active_pair_count[:, None]
    rows = jnp.where(live, pair_blocks[:, :, 0], -1).reshape(1, -1)
    cols = pair_blocks[:, :, 1].reshape(1, -1)
    match = rows == jnp.arange(blocks)[:, None]
    low = jnp.min(jnp.where(match, cols, blocks - 1), axis=1)
    high = jnp.max(jnp.where(match, cols, 0), axis=1)
    return jnp.stack([low, high], axis=1).reshape(-1).astype(jnp.int32)


def shared_slots(cols, blocks):
    tiles = jnp.arange(cols.shape[0])
    chip = cols // 2
    before = (chip[:, None] == chip[None, :]) & (tiles[None, :] < tiles[:, None])
    rank = jnp.sum(before.astype(jnp.int32), axis=1)
    device = 2 * chip + rank % 2
    slot = rank // 2
    entry = 1 + 2 * (tiles // 2) + (cols % 2 != rank % 2).astype(jnp.int32)
    place = device * SHARED + slot
    hit = (place[None, :] == jnp.arange(blocks * SHARED)[:, None]) & (slot[None, :] < SHARED)
    table = jnp.sum(jnp.where(hit, entry[None, :], 0), axis=1).astype(jnp.int32)
    return table.reshape(blocks, SHARED), jnp.max(rank)


def message_picks(cols, mine, me, blocks):
    source = jnp.arange(blocks * SUB) // SUB
    kind = (jnp.arange(blocks * SUB) % SUB) // 2
    pair = cols.reshape(blocks, 2)
    own_pair = lax.dynamic_index_in_dim(pair, me, 0, keepdims=False)
    columns = jnp.concatenate([jnp.stack([me, me ^ 1]).astype(jnp.int32), own_pair])[:, None]
    first = jnp.repeat(pair[:, 0], SUB)
    second = jnp.repeat(pair[:, 1], SUB)
    named = jnp.where(kind == 1, source, jnp.where(kind == 2, first, second))
    column_hit = (named[None, :] == columns) & (kind > 0)[None, :]
    row_blocks = jnp.concatenate([me.reshape(1).astype(jnp.int32), (mine + 1) // 2 - 1])[:, None]
    row_hit = (source[None, :] == row_blocks) & (kind == 0)[None, :]
    hits = jnp.concatenate([column_hit, row_hit], axis=0).astype(jnp.bfloat16)
    return jnp.pad(hits, ((0, PICKS - hits.shape[0]), (0, 0)))


def pieces(x):
    rows, features = x.shape
    tiled = x.reshape(rows // SUB, SUB, features // LANES, LANES).transpose(0, 2, 1, 3)
    return tiled.reshape(-1, SUB, LANES)


def fetch(cols, spread, query_unit):
    blocks = lax.axis_size("dp")
    wanted = vmem_call(
        first_gather_kernel, pltpu.VMEM((blocks, 3 * SUB, LANES), jnp.bfloat16), 1, 2, name="gather"
    )(cols, spread, pieces(query_unit))
    return exchange(wanted)


def general_path(query_emb, doc_emb, spread, cols, table, info, picks, own):
    qu, du, inv, _, et_own, _ = own
    fetched = fetch(cols, spread, qu)
    blocks = lax.axis_size("dp")
    rows, features = query_emb.shape
    row_tiles, col_tiles = rows // SUB, features // LANES
    sds = pltpu.VMEM
    bf16, f32 = jnp.bfloat16, jnp.float32
    send, et, row_total, dk = vmem_call(
        tiles_kernel,
        (
            sds((row_tiles, col_tiles, 5 * SUB, LANES), bf16),
            sds((2, rows, rows), f32),
            sds((1, rows), f32),
            sds((2, rows, features), bf16),
        ),
        0,
        3,
        name="tiles",
    )(qu, et_own, fetched)
    parts = exchange(send.reshape(blocks, 5 * SUB, LANES))
    acc = pltpu.VMEM((blocks, SUB, LANES), f32)
    combined = vmem_call(
        combine_kernel, sds((blocks, 2 * SUB, LANES), bf16), 1, 1, (acc, acc, acc), name="combine"
    )(cols, parts)
    home = exchange(combined)
    grad = jax.ShapeDtypeStruct((rows, features), f32)
    return vmem_call(final_kernel, (grad, grad), 0, 10, name="final")(
        query_emb, doc_emb, qu, du, inv, et_own, et, row_total, dk, home
    )


def short_path(shared, query_emb, doc_emb, spread, cols, table, info, picks, own):
    qu, du, inv, e_own, et_own, other = own
    fetched = fetch(cols, spread, qu)
    blocks = lax.axis_size("dp")
    rows, features = query_emb.shape
    assert rows == LANES
    sds = pltpu.VMEM
    bf16, f32 = jnp.bfloat16, jnp.float32
    wide = sds((rows, features), bf16)
    grad = jax.ShapeDtypeStruct((rows, features), f32)
    send, e, row_total, doc_units = vmem_call(
        row_side_kernel,
        (
            sds((blocks, (shared + 1) * SUB, LANES), bf16),
            sds((2, rows, rows), f32),
            sds((rows, 1), f32),
            sds((3 * rows, features), bf16),
        ),
        1,
        5,
        (pltpu.VMEM((SUB, LANES), bf16),),
        name="rows",
    )(table, qu, du, e_own, et_own, fetched)
    recv = exchange(send)
    acc, partner, sums = vmem_call(
        doc_side_kernel,
        (sds((rows, features), f32), wide, sds((PICKS, LANES), f32)),
        1,
        5,
        (
            pltpu.VMEM(((shared + 1) * rows, features), bf16),
            pltpu.VMEM((rows, features), bf16),
            pltpu.SemaphoreType.DMA,
        ),
        name="docs",
        n_any=1,
    )(info, other, picks, qu, du, et_own, recv)
    swapped = swap_cores(partner)
    grad_scratch = (pltpu.VMEM((rows, features), f32), pltpu.SemaphoreType.DMA((4,)))
    grad_query = vmem_call(
        query_side_kernel, grad, 0, 7, grad_scratch, name="queries", out_space=pl.ANY
    )(sums, query_emb, inv, e_own, e, row_total, doc_units)
    grad_doc = vmem_call(
        doc_final_kernel, grad, 0, 4, grad_scratch, name="final", out_space=pl.ANY
    )(doc_emb, inv, acc, swapped)
    return grad_query, grad_doc


def swap_cores(x):
    return lax.ppermute(x, "dp", [(i, i ^ 1) for i in range(lax.axis_size("dp"))])


def on_device(query_emb, doc_emb, pair_blocks, active_pair_count):
    blocks = lax.axis_size("dp")
    me = lax.axis_index("dp")
    rows, features = query_emb.shape
    row_tiles, col_tiles = rows // SUB, features // LANES
    assert row_tiles * col_tiles == blocks

    spread = exchange(pieces(doc_emb))
    cols = row_columns(pair_blocks, active_pair_count, blocks)
    mat, wide = pltpu.VMEM((rows, rows), jnp.float32), pltpu.VMEM((rows, features), jnp.bfloat16)
    own = vmem_call(
        own_pair_kernel, (wide, wide, pltpu.VMEM((rows, 2), jnp.float32), mat, mat), 0, 2, name="own", keep=False
    )(query_emb, doc_emb)
    own = (*own, swap_cores(own[1]))
    table, deepest = shared_slots(cols, blocks)
    info = lax.dynamic_index_in_dim(table, me, 0, keepdims=False)
    picks = message_picks(cols, info, me, blocks)
    table = (jnp.maximum(table - 1, 0) // 2).reshape(-1)
    choice = sum((deepest >= 2 * shared).astype(jnp.int32) for shared in CHOICES)
    spread, cols, table, info, picks, choice, own = lax.optimization_barrier(
        (spread, cols, table, info, picks, choice, own)
    )
    args = (query_emb, doc_emb, spread, cols, table, info, picks, own)
    paths = [functools.partial(short_path, shared) for shared in CHOICES] + [general_path]
    return lax.switch(choice, paths, *args)


def solution(mesh):
    return jax.shard_map(
        on_device,
        mesh=mesh,
        in_specs=(P("dp", None), P("dp", None), P(), P()),
        out_specs=(P("dp", None), P("dp", None)),
        check_vma=False,
    )
```

```python
import functools

import jax
import jax.numpy as jnp
from jax import lax
from jax.experimental import pallas as pl
from jax.experimental.pallas import tpu as pltpu
from jax.sharding import PartitionSpec as P

LOGIT_SCALE = 64.0
EPSILON = 1e-06
LANES = 128
SUB = 8
SHARED = 6
PICKS = 16
CHOICES = (4, 5, 6)
VMEM_BYTES = 16 * 1024 * 1024


def whole(space):
    return pl.BlockSpec(memory_space=space)


def vmem_call(body, outs, n_smem, n_vmem, scratch=(), name=None, n_any=0, out_space=pltpu.VMEM, keep=True):
    call = pl.pallas_call(
        body,
        out_shape=outs,
        in_specs=[whole(pltpu.SMEM)] * n_smem + [whole(pl.ANY)] * n_any + [whole(pltpu.VMEM)] * n_vmem,
        out_specs=jax.tree.map(lambda _: whole(out_space), outs),
        scratch_shapes=list(scratch),
        compiler_params=pltpu.CompilerParams(vmem_limit_bytes=VMEM_BYTES),
        name=name,
    )

    def run(*args):
        if not keep:
            return call(*args)
        kept = [pltpu.with_memory_space_constraint(x, pltpu.VMEM) for x in args[n_smem + n_any :]]
        return call(*args[: n_smem + n_any], *kept)

    return run


def inverse_norm(wide):
    return lax.rsqrt(jnp.sum(wide * wide, axis=1, keepdims=True) + EPSILON)


def from_pieces(pieces, slot):
    row_tiles, col_tiles = pieces.shape[:2]
    return jnp.concatenate(
        [pieces[:, ct, slot].reshape(row_tiles * SUB, LANES) for ct in range(col_tiles)], axis=1
    )


def dot_nt(a, b):
    return lax.dot_general(a, b, (((1,), (1,)), ((), ())), preferred_element_type=jnp.float32)


def dot_tn(a, b):
    return lax.dot_general(a, b, (((0,), (0,)), ((), ())), preferred_element_type=jnp.float32)


def dot_nn(a, b):
    return lax.dot_general(a, b, (((1,), (0,)), ((), ())), preferred_element_type=jnp.float32)


def own_kernel(q_ref, d_ref, qu_ref, du_ref, inv_ref, et_ref):
    q_wide = q_ref[...].astype(jnp.float32)
    d_wide = d_ref[...].astype(jnp.float32)
    q_inv = inverse_norm(q_wide)
    d_inv = inverse_norm(d_wide)
    q = (q_wide * q_inv).astype(jnp.bfloat16)
    d = (d_wide * d_inv).astype(jnp.bfloat16)
    qu_ref[...] = q
    du_ref[...] = d
    lane = lax.broadcasted_iota(jnp.int32, inv_ref.shape, 1)
    inv_ref[...] = jnp.where(lane == 0, q_inv, d_inv)
    et_ref[...] = jnp.exp(LOGIT_SCALE * dot_nt(d, q))


def split_pair(value, odd):
    high = value.astype(jnp.bfloat16).astype(jnp.float32)
    return jnp.where(odd, value - high, high)


def tiles_kernel(qu_ref, et_own_ref, fetched_ref, send_ref, et_ref, row_ref, dk_ref):
    row_tiles, col_tiles = send_ref.shape[:2]
    q = qu_ref[...]
    pieces = fetched_ref[:, 0 : 2 * SUB, :].astype(jnp.float32)
    pieces = pieces.reshape(row_tiles, col_tiles, 2, SUB, LANES)
    et_own = et_own_ref[...]
    row_total = jnp.sum(et_own, axis=0, keepdims=True)
    col_own = jnp.sum(et_own, axis=1, keepdims=True)
    ets, cols = [], []
    for k in range(2):
        wide = from_pieces(pieces, k)
        unit = (wide * inverse_norm(wide)).astype(jnp.bfloat16)
        dk_ref[k] = unit
        et = jnp.exp(LOGIT_SCALE * dot_nt(unit, q))
        et_ref[k] = et
        row_total = row_total + jnp.sum(et, axis=0, keepdims=True)
        cols.append(jnp.sum(et, axis=1, keepdims=True))
        ets.append(et)
    row_ref[...] = row_total
    row_inv = 1.0 / row_total
    half = 0.5 * LOGIT_SCALE
    parts = []
    for make in (lambda e: e * row_inv, lambda e: e):
        parts.append([half * dot_nn(make(e).astype(jnp.bfloat16), q) for e in ets])
    for ct in range(col_tiles):
        lanes = slice(ct * LANES, (ct + 1) * LANES)
        for kind in range(2):
            pair = [x[:, lanes].reshape(row_tiles, 1, SUB, LANES) for x in parts[kind]]
            both = jnp.concatenate(pair, axis=1).reshape(row_tiles, 2 * SUB, LANES)
            send_ref[:, ct, 2 * SUB * kind : 2 * SUB * (kind + 1), :] = both.astype(jnp.bfloat16)
    rows = row_tiles * SUB
    lane = lax.broadcasted_iota(jnp.int32, (rows, LANES), 1)
    value = jnp.where(lane < 2, col_own, jnp.where(lane < 4, cols[0], cols[1]))
    scalars = split_pair(value, lane % 2 == 1).reshape(row_tiles, SUB, LANES).astype(jnp.bfloat16)
    for ct in range(col_tiles):
        send_ref[:, ct, 4 * SUB :, :] = scalars


def combine_kernel(cols_ref, recv_ref, out_ref, acc_a, acc_b, acc_t):
    blocks = recv_ref.shape[0]
    acc_a[...] = jnp.zeros_like(acc_a)
    acc_b[...] = jnp.zeros_like(acc_b)
    lane3 = lax.broadcasted_iota(jnp.int32, acc_t.shape, 2)
    own = recv_ref[:, 4 * SUB :, :].astype(jnp.float32)
    acc_t[...] = jnp.where(lane3 < 2, own, 0.0)
    lane = lax.broadcasted_iota(jnp.int32, (SUB, LANES), 1)
    masks = [(lane >= 2) & (lane < 4), (lane >= 4) & (lane < 6)]

    def add(source, carry):
        a = recv_ref[source, 0 : 2 * SUB, :].astype(jnp.float32)
        b = recv_ref[source, 2 * SUB : 4 * SUB, :].astype(jnp.float32)
        t = recv_ref[source, 4 * SUB :, :].astype(jnp.float32)
        for k in range(2):
            col = cols_ref[2 * source + k]
            acc_a[col] = acc_a[col] + a[k * SUB : (k + 1) * SUB]
            acc_b[col] = acc_b[col] + b[k * SUB : (k + 1) * SUB]
            acc_t[col] = acc_t[col] + jnp.where(masks[k], t, 0.0)
        return carry

    lax.fori_loop(0, blocks, add, 0, unroll=8)
    total = jnp.broadcast_to(jnp.sum(acc_t[...], axis=2, keepdims=True), acc_t.shape)
    acc_t[...] = total
    acc_a[...] = acc_a[...] + acc_b[...] / total
    odd = lane % 2 == 1

    def emit(dest, carry):
        value = jnp.where(
            lane < 2,
            acc_t[dest],
            jnp.where(lane < 4, acc_t[cols_ref[2 * dest]], acc_t[cols_ref[2 * dest + 1]]),
        )
        both = jnp.concatenate([acc_a[dest], split_pair(value, odd)], axis=0)
        out_ref[dest] = both.astype(jnp.bfloat16)
        return carry

    lax.fori_loop(0, blocks, emit, 0, unroll=8)


def unit_grad(wide, inverse, upstream):
    radial = jnp.sum(wide * upstream, axis=1, keepdims=True)
    return upstream * inverse - wide * (radial * inverse * inverse * inverse)


def final_kernel(
    q_ref, d_ref, qu_ref, du_ref, inv_ref, et_own_ref, et_ref, row_ref, dk_ref, home_ref, gq_ref, gd_ref
):
    rows, features = q_ref.shape
    row_tiles, col_tiles = rows // SUB, features // LANES
    pieces = home_ref[...].astype(jnp.float32).reshape(row_tiles, col_tiles, 2, SUB, LANES)
    scalars = pieces[:, 0, 1].reshape(rows, LANES)
    totals = [scalars[:, 2 * i : 2 * i + 1] + scalars[:, 2 * i + 1 : 2 * i + 2] for i in range(3)]
    row_inv = 1.0 / row_ref[...]

    def weight(et, total):
        return 0.5 * (et * row_inv + et * (1.0 / total))

    own = weight(et_own_ref[...], totals[0])
    diagonal = lax.broadcasted_iota(jnp.int32, own.shape, 0) == lax.broadcasted_iota(
        jnp.int32, own.shape, 1
    )
    own = (own - jnp.where(diagonal, 1.0, 0.0)).astype(jnp.bfloat16)

    def part(x):
        return (LOGIT_SCALE * x).astype(jnp.bfloat16).astype(jnp.float32)

    query = part(dot_tn(own, du_ref[...]))
    for k in range(2):
        w = weight(et_ref[k], totals[k + 1]).astype(jnp.bfloat16)
        query = query + part(dot_tn(w, dk_ref[k]))
    gq_ref[...] = unit_grad(q_ref[...].astype(jnp.float32), inv_ref[:, 0:1], query)
    doc = part(dot_nn(own, qu_ref[...])) + from_pieces(pieces, 0)
    gd_ref[...] = unit_grad(d_ref[...].astype(jnp.float32), inv_ref[:, 1:2], doc)


def first_gather_kernel(cols_any, spread_ref, query_ref, out_ref, cols_ref, sem):
    bring = pltpu.make_async_copy(cols_any, cols_ref, sem)
    bring.start()
    out_ref[:, 2 * SUB :, :] = query_ref[...]
    bring.wait()

    def step(dest, carry):
        tiles = [spread_ref[cols_ref[2 * dest + k]] for k in range(2)]
        for slot, tile in enumerate(tiles):
            out_ref[dest, slot * SUB : (slot + 1) * SUB, :] = tile
        return carry

    lax.fori_loop(0, out_ref.shape[0], step, 0, unroll=16)


def eye_mask(n):
    return lax.broadcasted_iota(jnp.int32, (n, n), 0) == lax.broadcasted_iota(jnp.int32, (n, n), 1)


def to_lanes(column, eye):
    return jnp.sum(jnp.where(eye, column, 0.0), axis=0, keepdims=True)


def to_sublanes(row, eye):
    return jnp.sum(jnp.where(eye, row, 0.0), axis=1, keepdims=True)


def own_pair_kernel(q_ref, d_ref, qu_ref, du_ref, inv_ref, e_ref, et_ref):
    own_kernel(q_ref, d_ref, qu_ref, du_ref, inv_ref, et_ref)
    e_ref[...] = jnp.exp(LOGIT_SCALE * dot_nt(qu_ref[...], du_ref[...]))


def fetched_rows(fetched_ref, slot, row_tiles, col_tiles):
    piece = fetched_ref[:, slot * SUB : (slot + 1) * SUB, :].astype(jnp.float32)
    return from_pieces(piece.reshape(row_tiles, col_tiles, 1, SUB, LANES), 0)


def row_side_kernel(
    table_any, qu_ref, du_ref, e_own_ref, et_own_ref, fetched_ref,
    send_ref, e_ref, row_ref, units_ref, extra_ref, table_ref, sem
):
    bring = pltpu.make_async_copy(table_any, table_ref, sem)
    bring.start()
    rows, features = qu_ref.shape
    row_tiles, col_tiles = rows // SUB, features // LANES
    shared = send_ref.shape[1] // SUB - 1
    stride = table_ref.shape[0] // send_ref.shape[0]
    eye = eye_mask(rows)
    q = qu_ref[...]
    units_ref[0:rows] = du_ref[...]
    row_total = jnp.sum(e_own_ref[...], axis=1, keepdims=True)
    columns = [to_lanes(jnp.sum(et_own_ref[...], axis=1, keepdims=True), eye)]
    for k in range(2):
        piece = fetched_ref[...].reshape(row_tiles, col_tiles, 3, SUB, LANES)[:, :, k : k + 1]
        wide = from_pieces(piece.astype(jnp.float32), 0)
        unit = (wide * inverse_norm(wide)).astype(jnp.bfloat16)
        units_ref[(k + 1) * rows : (k + 2) * rows] = unit
        e = jnp.exp(LOGIT_SCALE * dot_nt(q, unit))
        e_ref[k] = e
        row_total = row_total + jnp.sum(e, axis=1, keepdims=True)
        columns.append(jnp.sum(e, axis=0, keepdims=True))
    row_ref[...] = row_total
    doubled = []
    for x in [to_lanes(row_total, eye)] + columns:
        high = x.astype(jnp.bfloat16).astype(jnp.float32)
        doubled += [high, x - high]
    extra_ref[...] = jnp.concatenate(doubled, axis=0).astype(jnp.bfloat16)
    send_ref[:, shared * SUB :, :] = jnp.broadcast_to(extra_ref[...][None], (send_ref.shape[0], SUB, LANES))

    bring.wait()

    def step(dest, carry):
        tiles = [fetched_ref[table_ref[dest * stride + slot]] for slot in range(shared)]
        for slot, tile in enumerate(tiles):
            send_ref[dest, slot * SUB : (slot + 1) * SUB, :] = tile
        return carry

    lax.fori_loop(0, send_ref.shape[0], step, 0, unroll=4)


def doc_side_kernel(
    info_any, other_any, pick_ref, qu_ref, du_ref, et_own_ref, recv_ref,
    acc_ref, partner_ref, sums_ref, units_ref, other_ref, sem, info_ref, info_sem
):
    bring = pltpu.make_async_copy(other_any, other_ref, sem)
    bring.start()
    bring_info = pltpu.make_async_copy(info_any, info_ref, info_sem)
    bring_info.start()
    rows, features = qu_ref.shape
    row_tiles, col_tiles = rows // SUB, features // LANES
    blocks = recv_ref.shape[0]
    shared = recv_ref.shape[1] // SUB - 1
    eye = eye_mask(rows)
    messages = recv_ref[:, shared * SUB :, :].astype(jnp.float32).reshape(blocks * SUB, LANES)
    sums = dot_nn(pick_ref[...], messages.astype(jnp.bfloat16))
    sums_ref[...] = sums
    inverse = [1.0 / to_sublanes(sums[i : i + 1], eye) for i in range(2)]

    def weight(et, row_total, col_inverse):
        return 0.5 * (et * (1.0 / row_total) + et * col_inverse)

    q = qu_ref[...]
    own = weight(et_own_ref[...], sums[4:5], inverse[0]) - jnp.where(eye, 1.0, 0.0)
    units_ref[0:rows] = q
    weights = [[own.astype(jnp.bfloat16)], [jnp.zeros((rows, rows), jnp.bfloat16)]]
    bring.wait()
    bring_info.wait()
    for slot in range(shared):
        entry = info_ref[slot]
        side = 1 - lax.rem(entry, 2)
        unit = fetched_rows(recv_ref, slot, row_tiles, col_tiles).astype(jnp.bfloat16)
        units_ref[(slot + 1) * rows : (slot + 2) * rows] = unit
        docs = jnp.where(side == 1, other_ref[...], du_ref[...])
        et = jnp.exp(LOGIT_SCALE * dot_nt(docs, unit))
        live = entry > 0
        total = jnp.where(live, sums[5 + slot : 6 + slot], 1.0)
        w = weight(et, total, jnp.where(side == 1, inverse[1], inverse[0]))
        for i in range(2):
            weights[i].append(jnp.where(live & (side == i), w, 0.0).astype(jnp.bfloat16))
    weights = jnp.concatenate([jnp.concatenate(w, axis=1) for w in weights], axis=0)
    grads = LOGIT_SCALE * dot_nn(weights, units_ref[...])
    acc_ref[...] = grads[0:rows]
    partner_ref[...] = grads[rows:].astype(jnp.bfloat16)


def query_side_kernel(sums_ref, q_ref, inv_ref, e_own_ref, e_ref, row_ref, units_ref, gq_ref, buf, sems):
    eye = eye_mask(q_ref.shape[0])
    row_inv = 1.0 / row_ref[...]

    def weight(e, which):
        return 0.5 * (e * row_inv + e * (1.0 / sums_ref[which : which + 1, :]))

    weights = [weight(e_own_ref[...], 0) - jnp.where(eye, 1.0, 0.0)]
    weights += [weight(e_ref[k], 2 + k) for k in range(2)]
    query = LOGIT_SCALE * dot_nn(jnp.concatenate(weights, axis=1).astype(jnp.bfloat16), units_ref[...])
    write_grad(gq_ref, buf, sems, lambda some: (q_ref[some], inv_ref[some, 0:1], query[some]))


def write_grad(out_ref, buf, sems, rows_of):
    parts = sems.shape[0]
    step = buf.shape[0] // parts
    copies = []
    for j in range(parts):
        some = slice(j * step, (j + 1) * step)
        raw, inverse, upstream = rows_of(some)
        buf[some] = unit_grad(raw.astype(jnp.float32), inverse, upstream)
        at = pl.ds(j * step, step)
        copies.append(pltpu.make_async_copy(buf.at[at], out_ref.at[at], sems.at[j]))
        copies[-1].start()
    for copy in copies:
        copy.wait()


def doc_final_kernel(d_ref, inv_ref, acc_ref, swapped_ref, gd_ref, buf, sems):
    def rows_of(some):
        return d_ref[some], inv_ref[some, 1:2], acc_ref[some] + swapped_ref[some].astype(jnp.float32)

    write_grad(gd_ref, buf, sems, rows_of)


def exchange(x):
    return lax.all_to_all(x, "dp", split_axis=0, concat_axis=0, tiled=True)


def row_columns(pair_blocks, active_pair_count, blocks):
    slots = pair_blocks.shape[1]
    live = jnp.arange(slots)[None, :] < active_pair_count[:, None]
    rows = jnp.where(live, pair_blocks[:, :, 0], -1).reshape(1, -1)
    cols = pair_blocks[:, :, 1].reshape(1, -1)
    match = rows == jnp.arange(blocks)[:, None]
    low = jnp.min(jnp.where(match, cols, blocks - 1), axis=1)
    high = jnp.max(jnp.where(match, cols, 0), axis=1)
    return jnp.stack([low, high], axis=1).reshape(-1).astype(jnp.int32)


def shared_slots(cols, blocks):
    tiles = jnp.arange(cols.shape[0])
    chip = cols // 2
    before = (chip[:, None] == chip[None, :]) & (tiles[None, :] < tiles[:, None])
    rank = jnp.sum(before.astype(jnp.int32), axis=1)
    device = 2 * chip + rank % 2
    slot = rank // 2
    entry = 1 + 2 * (tiles // 2) + (cols % 2 != rank % 2).astype(jnp.int32)
    place = device * SHARED + slot
    hit = (place[None, :] == jnp.arange(blocks * SHARED)[:, None]) & (slot[None, :] < SHARED)
    table = jnp.sum(jnp.where(hit, entry[None, :], 0), axis=1).astype(jnp.int32)
    return table.reshape(blocks, SHARED), jnp.max(rank)


def message_picks(cols, mine, me, blocks):
    source = jnp.arange(blocks * SUB) // SUB
    kind = (jnp.arange(blocks * SUB) % SUB) // 2
    pair = cols.reshape(blocks, 2)
    own_pair = lax.dynamic_index_in_dim(pair, me, 0, keepdims=False)
    columns = jnp.concatenate([jnp.stack([me, me ^ 1]).astype(jnp.int32), own_pair])[:, None]
    first = jnp.repeat(pair[:, 0], SUB)
    second = jnp.repeat(pair[:, 1], SUB)
    named = jnp.where(kind == 1, source, jnp.where(kind == 2, first, second))
    column_hit = (named[None, :] == columns) & (kind > 0)[None, :]
    row_blocks = jnp.concatenate([me.reshape(1).astype(jnp.int32), (mine + 1) // 2 - 1])[:, None]
    row_hit = (source[None, :] == row_blocks) & (kind == 0)[None, :]
    hits = jnp.concatenate([column_hit, row_hit], axis=0).astype(jnp.bfloat16)
    return jnp.pad(hits, ((0, PICKS - hits.shape[0]), (0, 0)))


def pieces(x):
    rows, features = x.shape
    tiled = x.reshape(rows // SUB, SUB, features // LANES, LANES).transpose(0, 2, 1, 3)
    return tiled.reshape(-1, SUB, LANES)


def small_table(x):
    return pltpu.SMEM(x.shape, x.dtype), pltpu.SemaphoreType.DMA


def fetch(cols, spread, query_unit):
    blocks = lax.axis_size("dp")
    wanted = vmem_call(
        first_gather_kernel,
        pltpu.VMEM((blocks, 3 * SUB, LANES), jnp.bfloat16),
        0,
        2,
        small_table(cols),
        name="gather",
        n_any=1,
    )(cols, spread, pieces(query_unit))
    return exchange(wanted)


def general_path(query_emb, doc_emb, spread, cols, table, info, picks, own):
    qu, du, inv, _, et_own, _ = own
    fetched = fetch(cols, spread, qu)
    blocks = lax.axis_size("dp")
    rows, features = query_emb.shape
    row_tiles, col_tiles = rows // SUB, features // LANES
    sds = pltpu.VMEM
    bf16, f32 = jnp.bfloat16, jnp.float32
    send, et, row_total, dk = vmem_call(
        tiles_kernel,
        (
            sds((row_tiles, col_tiles, 5 * SUB, LANES), bf16),
            sds((2, rows, rows), f32),
            sds((1, rows), f32),
            sds((2, rows, features), bf16),
        ),
        0,
        3,
        name="tiles",
    )(qu, et_own, fetched)
    parts = exchange(send.reshape(blocks, 5 * SUB, LANES))
    acc = pltpu.VMEM((blocks, SUB, LANES), f32)
    combined = vmem_call(
        combine_kernel, sds((blocks, 2 * SUB, LANES), bf16), 1, 1, (acc, acc, acc), name="combine"
    )(cols, parts)
    home = exchange(combined)
    grad = jax.ShapeDtypeStruct((rows, features), f32)
    return vmem_call(final_kernel, (grad, grad), 0, 10, name="final")(
        query_emb, doc_emb, qu, du, inv, et_own, et, row_total, dk, home
    )


def short_path(shared, query_emb, doc_emb, spread, cols, table, info, picks, own):
    qu, du, inv, e_own, et_own, other = own
    fetched = fetch(cols, spread, qu)
    blocks = lax.axis_size("dp")
    rows, features = query_emb.shape
    assert rows == LANES
    sds = pltpu.VMEM
    bf16, f32 = jnp.bfloat16, jnp.float32
    wide = sds((rows, features), bf16)
    grad = jax.ShapeDtypeStruct((rows, features), f32)
    send, e, row_total, doc_units = vmem_call(
        row_side_kernel,
        (
            sds((blocks, (shared + 1) * SUB, LANES), bf16),
            sds((2, rows, rows), f32),
            sds((rows, 1), f32),
            sds((3 * rows, features), bf16),
        ),
        0,
        5,
        (pltpu.VMEM((SUB, LANES), bf16), *small_table(table)),
        name="rows",
        n_any=1,
    )(table, qu, du, e_own, et_own, fetched.reshape(3 * blocks, SUB, LANES))
    recv = exchange(send)
    acc, partner, sums = vmem_call(
        doc_side_kernel,
        (sds((rows, features), f32), wide, sds((PICKS, LANES), f32)),
        0,
        5,
        (
            pltpu.VMEM(((shared + 1) * rows, features), bf16),
            pltpu.VMEM((rows, features), bf16),
            pltpu.SemaphoreType.DMA,
            *small_table(info),
        ),
        name="docs",
        n_any=2,
    )(info, other, picks, qu, du, et_own, recv)
    swapped = swap_cores(partner)
    grad_scratch = (pltpu.VMEM((rows, features), f32), pltpu.SemaphoreType.DMA((4,)))
    grad_query = vmem_call(
        query_side_kernel, grad, 0, 7, grad_scratch, name="queries", out_space=pl.ANY
    )(sums, query_emb, inv, e_own, e, row_total, doc_units)
    grad_doc = vmem_call(
        doc_final_kernel, grad, 0, 4, grad_scratch, name="final", out_space=pl.ANY
    )(doc_emb, inv, acc, swapped)
    return grad_query, grad_doc


def swap_cores(x):
    return lax.ppermute(x, "dp", [(i, i ^ 1) for i in range(lax.axis_size("dp"))])


def on_device(query_emb, doc_emb, pair_blocks, active_pair_count):
    blocks = lax.axis_size("dp")
    me = lax.axis_index("dp")
    rows, features = query_emb.shape
    row_tiles, col_tiles = rows // SUB, features // LANES
    assert row_tiles * col_tiles == blocks

    spread = exchange(pieces(doc_emb))
    cols = row_columns(pair_blocks, active_pair_count, blocks)
    mat, wide = pltpu.VMEM((rows, rows), jnp.float32), pltpu.VMEM((rows, features), jnp.bfloat16)
    own = vmem_call(
        own_pair_kernel, (wide, wide, pltpu.VMEM((rows, 2), jnp.float32), mat, mat), 0, 2, name="own", keep=False
    )(query_emb, doc_emb)
    own = (*own, swap_cores(own[1]))
    table, deepest = shared_slots(cols, blocks)
    info = lax.dynamic_index_in_dim(table, me, 0, keepdims=False)
    picks = message_picks(cols, info, me, blocks)
    table = jnp.pad(3 * (jnp.maximum(table - 1, 0) // 2) + 2, ((0, 0), (0, SUB - SHARED))).reshape(-1)
    info = jnp.pad(info, (0, LANES - SHARED))
    choice = sum((deepest >= 2 * shared).astype(jnp.int32) for shared in CHOICES)
    spread, cols, table, info, picks, choice, own = lax.optimization_barrier(
        (spread, cols, table, info, picks, choice, own)
    )
    args = (query_emb, doc_emb, spread, cols, table, info, picks, own)
    paths = [functools.partial(short_path, shared) for shared in CHOICES] + [general_path]
    return lax.switch(choice, paths, *args)


def solution(mesh):
    return jax.shard_map(
        on_device,
        mesh=mesh,
        in_specs=(P("dp", None), P("dp", None), P(), P()),
        out_specs=(P("dp", None), P("dp", None)),
        check_vma=False,
    )
```

```python
import functools

import jax
import jax.numpy as jnp
from jax import lax
from jax.experimental import pallas as pl
from jax.experimental.pallas import tpu as pltpu
from jax.sharding import PartitionSpec as P

LOGIT_SCALE = 64.0
EPSILON = 1e-06
LANES = 128
SUB = 8
SHARED = 6
PICKS = 16
CHOICES = (4, 5, 6)
VMEM_BYTES = 16 * 1024 * 1024


def whole(space):
    return pl.BlockSpec(memory_space=space)


def vmem_call(body, outs, n_smem, n_vmem, scratch=(), name=None, n_any=0, out_space=pltpu.VMEM, keep=True):
    call = pl.pallas_call(
        body,
        out_shape=outs,
        in_specs=[whole(pltpu.SMEM)] * n_smem + [whole(pl.ANY)] * n_any + [whole(pltpu.VMEM)] * n_vmem,
        out_specs=jax.tree.map(lambda _: whole(out_space), outs),
        scratch_shapes=list(scratch),
        compiler_params=pltpu.CompilerParams(vmem_limit_bytes=VMEM_BYTES),
        name=name,
    )

    def run(*args):
        if not keep:
            return call(*args)
        kept = [pltpu.with_memory_space_constraint(x, pltpu.VMEM) for x in args[n_smem + n_any :]]
        return call(*args[: n_smem + n_any], *kept)

    return run


def inverse_norm(wide):
    return lax.rsqrt(jnp.sum(wide * wide, axis=1, keepdims=True) + EPSILON)


def from_pieces(pieces, slot):
    row_tiles, col_tiles = pieces.shape[:2]
    return jnp.concatenate(
        [pieces[:, ct, slot].reshape(row_tiles * SUB, LANES) for ct in range(col_tiles)], axis=1
    )


def dot_nt(a, b):
    return lax.dot_general(a, b, (((1,), (1,)), ((), ())), preferred_element_type=jnp.float32)


def dot_tn(a, b):
    return lax.dot_general(a, b, (((0,), (0,)), ((), ())), preferred_element_type=jnp.float32)


def dot_nn(a, b):
    return lax.dot_general(a, b, (((1,), (0,)), ((), ())), preferred_element_type=jnp.float32)


def own_kernel(q_ref, d_ref, qu_ref, du_ref, inv_ref, et_ref):
    q_wide = q_ref[...].astype(jnp.float32)
    d_wide = d_ref[...].astype(jnp.float32)
    q_inv = inverse_norm(q_wide)
    d_inv = inverse_norm(d_wide)
    q = (q_wide * q_inv).astype(jnp.bfloat16)
    d = (d_wide * d_inv).astype(jnp.bfloat16)
    qu_ref[...] = q
    du_ref[...] = d
    lane = lax.broadcasted_iota(jnp.int32, inv_ref.shape, 1)
    inv_ref[...] = jnp.where(lane == 0, q_inv, d_inv)
    et_ref[...] = jnp.exp(LOGIT_SCALE * dot_nt(d, q))


def split_pair(value, odd):
    high = value.astype(jnp.bfloat16).astype(jnp.float32)
    return jnp.where(odd, value - high, high)


def tiles_kernel(qu_ref, et_own_ref, fetched_ref, send_ref, et_ref, row_ref, dk_ref):
    row_tiles, col_tiles = send_ref.shape[:2]
    q = qu_ref[...]
    pieces = fetched_ref[:, 0 : 2 * SUB, :].astype(jnp.float32)
    pieces = pieces.reshape(row_tiles, col_tiles, 2, SUB, LANES)
    et_own = et_own_ref[...]
    row_total = jnp.sum(et_own, axis=0, keepdims=True)
    col_own = jnp.sum(et_own, axis=1, keepdims=True)
    ets, cols = [], []
    for k in range(2):
        wide = from_pieces(pieces, k)
        unit = (wide * inverse_norm(wide)).astype(jnp.bfloat16)
        dk_ref[k] = unit
        et = jnp.exp(LOGIT_SCALE * dot_nt(unit, q))
        et_ref[k] = et
        row_total = row_total + jnp.sum(et, axis=0, keepdims=True)
        cols.append(jnp.sum(et, axis=1, keepdims=True))
        ets.append(et)
    row_ref[...] = row_total
    row_inv = 1.0 / row_total
    half = 0.5 * LOGIT_SCALE
    parts = []
    for make in (lambda e: e * row_inv, lambda e: e):
        parts.append([half * dot_nn(make(e).astype(jnp.bfloat16), q) for e in ets])
    for ct in range(col_tiles):
        lanes = slice(ct * LANES, (ct + 1) * LANES)
        for kind in range(2):
            pair = [x[:, lanes].reshape(row_tiles, 1, SUB, LANES) for x in parts[kind]]
            both = jnp.concatenate(pair, axis=1).reshape(row_tiles, 2 * SUB, LANES)
            send_ref[:, ct, 2 * SUB * kind : 2 * SUB * (kind + 1), :] = both.astype(jnp.bfloat16)
    rows = row_tiles * SUB
    lane = lax.broadcasted_iota(jnp.int32, (rows, LANES), 1)
    value = jnp.where(lane < 2, col_own, jnp.where(lane < 4, cols[0], cols[1]))
    scalars = split_pair(value, lane % 2 == 1).reshape(row_tiles, SUB, LANES).astype(jnp.bfloat16)
    for ct in range(col_tiles):
        send_ref[:, ct, 4 * SUB :, :] = scalars


def combine_kernel(cols_ref, recv_ref, out_ref, acc_a, acc_b, acc_t):
    blocks = recv_ref.shape[0]
    acc_a[...] = jnp.zeros_like(acc_a)
    acc_b[...] = jnp.zeros_like(acc_b)
    lane3 = lax.broadcasted_iota(jnp.int32, acc_t.shape, 2)
    own = recv_ref[:, 4 * SUB :, :].astype(jnp.float32)
    acc_t[...] = jnp.where(lane3 < 2, own, 0.0)
    lane = lax.broadcasted_iota(jnp.int32, (SUB, LANES), 1)
    masks = [(lane >= 2) & (lane < 4), (lane >= 4) & (lane < 6)]

    def add(source, carry):
        a = recv_ref[source, 0 : 2 * SUB, :].astype(jnp.float32)
        b = recv_ref[source, 2 * SUB : 4 * SUB, :].astype(jnp.float32)
        t = recv_ref[source, 4 * SUB :, :].astype(jnp.float32)
        for k in range(2):
            col = cols_ref[2 * source + k]
            acc_a[col] = acc_a[col] + a[k * SUB : (k + 1) * SUB]
            acc_b[col] = acc_b[col] + b[k * SUB : (k + 1) * SUB]
            acc_t[col] = acc_t[col] + jnp.where(masks[k], t, 0.0)
        return carry

    lax.fori_loop(0, blocks, add, 0, unroll=8)
    total = jnp.broadcast_to(jnp.sum(acc_t[...], axis=2, keepdims=True), acc_t.shape)
    acc_t[...] = total
    acc_a[...] = acc_a[...] + acc_b[...] / total
    odd = lane % 2 == 1

    def emit(dest, carry):
        value = jnp.where(
            lane < 2,
            acc_t[dest],
            jnp.where(lane < 4, acc_t[cols_ref[2 * dest]], acc_t[cols_ref[2 * dest + 1]]),
        )
        both = jnp.concatenate([acc_a[dest], split_pair(value, odd)], axis=0)
        out_ref[dest] = both.astype(jnp.bfloat16)
        return carry

    lax.fori_loop(0, blocks, emit, 0, unroll=8)


def unit_grad(wide, inverse, upstream):
    radial = jnp.sum(wide * upstream, axis=1, keepdims=True)
    return upstream * inverse - wide * (radial * inverse * inverse * inverse)


def final_kernel(
    q_ref, d_ref, qu_ref, du_ref, inv_ref, et_own_ref, et_ref, row_ref, dk_ref, home_ref, gq_ref, gd_ref
):
    rows, features = q_ref.shape
    row_tiles, col_tiles = rows // SUB, features // LANES
    pieces = home_ref[...].astype(jnp.float32).reshape(row_tiles, col_tiles, 2, SUB, LANES)
    scalars = pieces[:, 0, 1].reshape(rows, LANES)
    totals = [scalars[:, 2 * i : 2 * i + 1] + scalars[:, 2 * i + 1 : 2 * i + 2] for i in range(3)]
    row_inv = 1.0 / row_ref[...]

    def weight(et, total):
        return 0.5 * (et * row_inv + et * (1.0 / total))

    own = weight(et_own_ref[...], totals[0])
    diagonal = lax.broadcasted_iota(jnp.int32, own.shape, 0) == lax.broadcasted_iota(
        jnp.int32, own.shape, 1
    )
    own = (own - jnp.where(diagonal, 1.0, 0.0)).astype(jnp.bfloat16)

    def part(x):
        return (LOGIT_SCALE * x).astype(jnp.bfloat16).astype(jnp.float32)

    query = part(dot_tn(own, du_ref[...]))
    for k in range(2):
        w = weight(et_ref[k], totals[k + 1]).astype(jnp.bfloat16)
        query = query + part(dot_tn(w, dk_ref[k]))
    gq_ref[...] = unit_grad(q_ref[...].astype(jnp.float32), inv_ref[:, 0:1], query)
    doc = part(dot_nn(own, qu_ref[...])) + from_pieces(pieces, 0)
    gd_ref[...] = unit_grad(d_ref[...].astype(jnp.float32), inv_ref[:, 1:2], doc)


def first_gather_kernel(cols_any, spread_ref, query_ref, out_ref, cols_ref, sem):
    bring = pltpu.make_async_copy(cols_any, cols_ref, sem)
    bring.start()
    out_ref[:, 2 * SUB :, :] = query_ref[...]
    bring.wait()

    def step(dest, carry):
        tiles = [spread_ref[cols_ref[2 * dest + k]] for k in range(2)]
        for slot, tile in enumerate(tiles):
            out_ref[dest, slot * SUB : (slot + 1) * SUB, :] = tile
        return carry

    lax.fori_loop(0, out_ref.shape[0], step, 0, unroll=16)


def eye_mask(n):
    return lax.broadcasted_iota(jnp.int32, (n, n), 0) == lax.broadcasted_iota(jnp.int32, (n, n), 1)


def to_lanes(column, eye):
    return jnp.sum(jnp.where(eye, column, 0.0), axis=0, keepdims=True)


def to_sublanes(row, eye):
    return jnp.sum(jnp.where(eye, row, 0.0), axis=1, keepdims=True)


def own_pair_kernel(q_ref, d_ref, qu_ref, du_ref, inv_ref, e_ref, et_ref):
    own_kernel(q_ref, d_ref, qu_ref, du_ref, inv_ref, et_ref)
    e_ref[...] = jnp.exp(LOGIT_SCALE * dot_nt(qu_ref[...], du_ref[...]))


def fetched_rows(fetched_ref, slot, row_tiles, col_tiles):
    piece = fetched_ref[:, slot * SUB : (slot + 1) * SUB, :].astype(jnp.float32)
    return from_pieces(piece.reshape(row_tiles, col_tiles, 1, SUB, LANES), 0)


def row_side_kernel(
    table_any, qu_ref, du_ref, e_own_ref, et_own_ref, fetched_ref,
    send_ref, e_ref, row_ref, units_ref, extra_ref, table_ref, sem
):
    bring = pltpu.make_async_copy(table_any, table_ref, sem)
    bring.start()
    rows, features = qu_ref.shape
    row_tiles, col_tiles = rows // SUB, features // LANES
    shared = send_ref.shape[1] // SUB - 1
    stride = table_ref.shape[0] // send_ref.shape[0]
    eye = eye_mask(rows)
    q = qu_ref[...]
    units_ref[0:rows] = du_ref[...]
    row_total = jnp.sum(e_own_ref[...], axis=1, keepdims=True)
    columns = [to_lanes(jnp.sum(et_own_ref[...], axis=1, keepdims=True), eye)]
    for k in range(2):
        piece = fetched_ref[...].reshape(row_tiles, col_tiles, 3, SUB, LANES)[:, :, k : k + 1]
        wide = from_pieces(piece.astype(jnp.float32), 0)
        unit = (wide * inverse_norm(wide)).astype(jnp.bfloat16)
        units_ref[(k + 1) * rows : (k + 2) * rows] = unit
        e = jnp.exp(LOGIT_SCALE * dot_nt(q, unit))
        e_ref[k] = e
        row_total = row_total + jnp.sum(e, axis=1, keepdims=True)
        columns.append(jnp.sum(e, axis=0, keepdims=True))
    row_ref[...] = row_total
    doubled = []
    for x in [to_lanes(row_total, eye)] + columns:
        high = x.astype(jnp.bfloat16).astype(jnp.float32)
        doubled += [high, x - high]
    extra_ref[...] = jnp.concatenate(doubled, axis=0).astype(jnp.bfloat16)
    send_ref[:, shared * SUB :, :] = jnp.broadcast_to(extra_ref[...][None], (send_ref.shape[0], SUB, LANES))

    bring.wait()

    def step(dest, carry):
        tiles = [fetched_ref[table_ref[dest * stride + slot]] for slot in range(shared)]
        for slot, tile in enumerate(tiles):
            send_ref[dest, slot * SUB : (slot + 1) * SUB, :] = tile
        return carry

    lax.fori_loop(0, send_ref.shape[0], step, 0, unroll=4)


def doc_side_kernel(
    info_any, other_any, pick_ref, qu_ref, du_ref, et_own_ref, recv_ref,
    acc_ref, partner_ref, sums_ref, units_ref, other_ref, sem, info_ref, info_sem
):
    bring = pltpu.make_async_copy(other_any, other_ref, sem)
    bring.start()
    bring_info = pltpu.make_async_copy(info_any, info_ref, info_sem)
    bring_info.start()
    rows, features = qu_ref.shape
    row_tiles, col_tiles = rows // SUB, features // LANES
    blocks = recv_ref.shape[0]
    shared = recv_ref.shape[1] // SUB - 1
    eye = eye_mask(rows)
    messages = recv_ref[:, shared * SUB :, :].astype(jnp.float32).reshape(blocks * SUB, LANES)
    sums = dot_nn(pick_ref[...], messages.astype(jnp.bfloat16))
    sums_ref[...] = sums
    inverse = [1.0 / to_sublanes(sums[i : i + 1], eye) for i in range(2)]

    def weight(et, row_total, col_inverse):
        return 0.5 * (et * (1.0 / row_total) + et * col_inverse)

    q = qu_ref[...]
    own = weight(et_own_ref[...], sums[4:5], inverse[0]) - jnp.where(eye, 1.0, 0.0)
    units_ref[0:rows] = q
    weights = [[own.astype(jnp.bfloat16)], [jnp.zeros((rows, rows), jnp.bfloat16)]]
    bring.wait()
    bring_info.wait()
    for slot in range(shared):
        entry = info_ref[slot]
        side = 1 - lax.rem(entry, 2)
        unit = fetched_rows(recv_ref, slot, row_tiles, col_tiles).astype(jnp.bfloat16)
        units_ref[(slot + 1) * rows : (slot + 2) * rows] = unit
        docs = jnp.where(side == 1, other_ref[...], du_ref[...])
        et = jnp.exp(LOGIT_SCALE * dot_nt(docs, unit))
        live = entry > 0
        total = jnp.where(live, sums[5 + slot : 6 + slot], 1.0)
        w = weight(et, total, jnp.where(side == 1, inverse[1], inverse[0]))
        for i in range(2):
            weights[i].append(jnp.where(live & (side == i), w, 0.0).astype(jnp.bfloat16))
    weights = jnp.concatenate([jnp.concatenate(w, axis=1) for w in weights], axis=0)
    grads = LOGIT_SCALE * dot_nn(weights, units_ref[...])
    acc_ref[...] = grads[0:rows]
    partner_ref[...] = grads[rows:].astype(jnp.bfloat16)


def query_side_kernel(sums_ref, q_ref, inv_ref, e_own_ref, e_ref, row_ref, units_ref, gq_ref, buf, sems):
    eye = eye_mask(q_ref.shape[0])
    row_inv = 1.0 / row_ref[...]

    def weight(e, which):
        return 0.5 * (e * row_inv + e * (1.0 / sums_ref[which : which + 1, :]))

    weights = [weight(e_own_ref[...], 0) - jnp.where(eye, 1.0, 0.0)]
    weights += [weight(e_ref[k], 2 + k) for k in range(2)]
    query = LOGIT_SCALE * dot_nn(jnp.concatenate(weights, axis=1).astype(jnp.bfloat16), units_ref[...])
    write_grad(gq_ref, buf, sems, lambda some: (q_ref[some], inv_ref[some, 0:1], query[some]))


def write_grad(out_ref, buf, sems, rows_of):
    parts = sems.shape[0]
    step = buf.shape[0] // parts
    copies = []
    for j in range(parts):
        some = slice(j * step, (j + 1) * step)
        raw, inverse, upstream = rows_of(some)
        buf[some] = unit_grad(raw.astype(jnp.float32), inverse, upstream)
        at = pl.ds(j * step, step)
        copies.append(pltpu.make_async_copy(buf.at[at], out_ref.at[at], sems.at[j]))
        copies[-1].start()
    for copy in copies:
        copy.wait()


def doc_final_kernel(d_ref, inv_ref, acc_ref, swapped_ref, gd_ref, buf, sems):
    def rows_of(some):
        return d_ref[some], inv_ref[some, 1:2], acc_ref[some] + swapped_ref[some].astype(jnp.float32)

    write_grad(gd_ref, buf, sems, rows_of)


def exchange(x):
    return lax.all_to_all(x, "dp", split_axis=0, concat_axis=0, tiled=True)


def row_columns(pair_blocks, active_pair_count, blocks):
    slots = pair_blocks.shape[1]
    live = jnp.arange(slots)[None, :] < active_pair_count[:, None]
    rows = jnp.where(live, pair_blocks[:, :, 0], -1).reshape(1, -1)
    cols = pair_blocks[:, :, 1].reshape(1, -1)
    match = rows == jnp.arange(blocks)[:, None]
    low = jnp.min(jnp.where(match, cols, blocks - 1), axis=1)
    high = jnp.max(jnp.where(match, cols, 0), axis=1)
    return jnp.stack([low, high], axis=1).reshape(-1).astype(jnp.int32)


def shared_slots(cols, blocks):
    tiles = jnp.arange(cols.shape[0])
    chip = cols // 2
    before = (chip[:, None] == chip[None, :]) & (tiles[None, :] < tiles[:, None])
    rank = jnp.sum(before.astype(jnp.int32), axis=1)
    device = 2 * chip + rank % 2
    slot = rank // 2
    entry = 1 + 2 * (tiles // 2) + (cols % 2 != rank % 2).astype(jnp.int32)
    place = device * SHARED + slot
    hit = (place[None, :] == jnp.arange(blocks * SHARED)[:, None]) & (slot[None, :] < SHARED)
    table = jnp.sum(jnp.where(hit, entry[None, :], 0), axis=1).astype(jnp.int32)
    level = sum((rank >= 2 * shared).astype(jnp.int32) for shared in CHOICES)
    return table.reshape(blocks, SHARED), jnp.max(level)


def message_picks(cols, mine, me, blocks):
    source = jnp.arange(blocks * SUB) // SUB
    kind = (jnp.arange(blocks * SUB) % SUB) // 2
    pair = cols.reshape(blocks, 2)
    own_pair = lax.dynamic_index_in_dim(pair, me, 0, keepdims=False)
    columns = jnp.concatenate([jnp.stack([me, me ^ 1]).astype(jnp.int32), own_pair])[:, None]
    first = jnp.repeat(pair[:, 0], SUB)
    second = jnp.repeat(pair[:, 1], SUB)
    named = jnp.where(kind == 1, source, jnp.where(kind == 2, first, second))
    column_hit = (named[None, :] == columns) & (kind > 0)[None, :]
    row_blocks = jnp.concatenate([me.reshape(1).astype(jnp.int32), (mine + 1) // 2 - 1])[:, None]
    row_hit = (source[None, :] == row_blocks) & (kind == 0)[None, :]
    hits = jnp.concatenate([column_hit, row_hit], axis=0).astype(jnp.bfloat16)
    return jnp.pad(hits, ((0, PICKS - hits.shape[0]), (0, 0)))


def pieces(x):
    rows, features = x.shape
    tiled = x.reshape(rows // SUB, SUB, features // LANES, LANES).transpose(0, 2, 1, 3)
    return tiled.reshape(-1, SUB, LANES)


def small_table(x):
    return pltpu.SMEM(x.shape, x.dtype), pltpu.SemaphoreType.DMA


def fetch(cols, spread, query_unit):
    blocks = lax.axis_size("dp")
    wanted = vmem_call(
        first_gather_kernel,
        pltpu.VMEM((blocks, 3 * SUB, LANES), jnp.bfloat16),
        0,
        2,
        small_table(cols),
        name="gather",
        n_any=1,
    )(cols, spread, pieces(query_unit))
    return exchange(wanted)


def general_path(query_emb, doc_emb, spread, cols, table, info, picks, own):
    qu, du, inv, _, et_own, _ = own
    fetched = fetch(cols, spread, qu)
    blocks = lax.axis_size("dp")
    rows, features = query_emb.shape
    row_tiles, col_tiles = rows // SUB, features // LANES
    sds = pltpu.VMEM
    bf16, f32 = jnp.bfloat16, jnp.float32
    send, et, row_total, dk = vmem_call(
        tiles_kernel,
        (
            sds((row_tiles, col_tiles, 5 * SUB, LANES), bf16),
            sds((2, rows, rows), f32),
            sds((1, rows), f32),
            sds((2, rows, features), bf16),
        ),
        0,
        3,
        name="tiles",
    )(qu, et_own, fetched)
    parts = exchange(send.reshape(blocks, 5 * SUB, LANES))
    acc = pltpu.VMEM((blocks, SUB, LANES), f32)
    combined = vmem_call(
        combine_kernel, sds((blocks, 2 * SUB, LANES), bf16), 1, 1, (acc, acc, acc), name="combine"
    )(cols, parts)
    home = exchange(combined)
    grad = jax.ShapeDtypeStruct((rows, features), f32)
    return vmem_call(final_kernel, (grad, grad), 0, 10, name="final")(
        query_emb, doc_emb, qu, du, inv, et_own, et, row_total, dk, home
    )


def short_path(shared, query_emb, doc_emb, spread, cols, table, info, picks, own):
    qu, du, inv, e_own, et_own, other = own
    fetched = fetch(cols, spread, qu)
    blocks = lax.axis_size("dp")
    rows, features = query_emb.shape
    assert rows == LANES
    sds = pltpu.VMEM
    bf16, f32 = jnp.bfloat16, jnp.float32
    wide = sds((rows, features), bf16)
    grad = jax.ShapeDtypeStruct((rows, features), f32)
    send, e, row_total, doc_units = vmem_call(
        row_side_kernel,
        (
            sds((blocks, (shared + 1) * SUB, LANES), bf16),
            sds((2, rows, rows), f32),
            sds((rows, 1), f32),
            sds((3 * rows, features), bf16),
        ),
        0,
        5,
        (pltpu.VMEM((SUB, LANES), bf16), *small_table(table)),
        name="rows",
        n_any=1,
    )(table, qu, du, e_own, et_own, fetched.reshape(3 * blocks, SUB, LANES))
    recv = exchange(send)
    acc, partner, sums = vmem_call(
        doc_side_kernel,
        (sds((rows, features), f32), wide, sds((PICKS, LANES), f32)),
        0,
        5,
        (
            pltpu.VMEM(((shared + 1) * rows, features), bf16),
            pltpu.VMEM((rows, features), bf16),
            pltpu.SemaphoreType.DMA,
            *small_table(info),
        ),
        name="docs",
        n_any=2,
    )(info, other, picks, qu, du, et_own, recv)
    swapped = swap_cores(partner)
    grad_scratch = (pltpu.VMEM((rows, features), f32), pltpu.SemaphoreType.DMA((4,)))
    grad_query = vmem_call(
        query_side_kernel, grad, 0, 7, grad_scratch, name="queries", out_space=pl.ANY
    )(sums, query_emb, inv, e_own, e, row_total, doc_units)
    grad_doc = vmem_call(
        doc_final_kernel, grad, 0, 4, grad_scratch, name="final", out_space=pl.ANY
    )(doc_emb, inv, acc, swapped)
    return grad_query, grad_doc


def swap_cores(x):
    return lax.ppermute(x, "dp", [(i, i ^ 1) for i in range(lax.axis_size("dp"))])


def on_device(query_emb, doc_emb, pair_blocks, active_pair_count):
    blocks = lax.axis_size("dp")
    me = lax.axis_index("dp")
    rows, features = query_emb.shape
    row_tiles, col_tiles = rows // SUB, features // LANES
    assert row_tiles * col_tiles == blocks

    spread = exchange(pieces(doc_emb))
    cols = row_columns(pair_blocks, active_pair_count, blocks)
    mat, wide = pltpu.VMEM((rows, rows), jnp.float32), pltpu.VMEM((rows, features), jnp.bfloat16)
    own = vmem_call(
        own_pair_kernel, (wide, wide, pltpu.VMEM((rows, 2), jnp.float32), mat, mat), 0, 2, name="own", keep=False
    )(query_emb, doc_emb)
    own = (*own, swap_cores(own[1]))
    table, choice = shared_slots(cols, blocks)
    info = lax.dynamic_index_in_dim(table, me, 0, keepdims=False)
    picks = message_picks(cols, info, me, blocks)
    table = jnp.pad(3 * (jnp.maximum(table - 1, 0) // 2) + 2, ((0, 0), (0, SUB - SHARED))).reshape(-1)
    info = jnp.pad(info, (0, LANES - SHARED))
    spread, cols, table, info, picks, choice, own = lax.optimization_barrier(
        (spread, cols, table, info, picks, choice, own)
    )
    args = (query_emb, doc_emb, spread, cols, table, info, picks, own)
    paths = [functools.partial(short_path, shared) for shared in CHOICES] + [general_path]
    return lax.switch(choice, paths, *args)


def solution(mesh):
    return jax.shard_map(
        on_device,
        mesh=mesh,
        in_specs=(P("dp", None), P("dp", None), P(), P()),
        out_specs=(P("dp", None), P("dp", None)),
        check_vma=False,
    )
```

```python
import functools

import jax
import jax.numpy as jnp
from jax import lax
from jax.experimental import pallas as pl
from jax.experimental.pallas import tpu as pltpu
from jax.sharding import PartitionSpec as P

LOGIT_SCALE = 64.0
EPSILON = 1e-06
LANES = 128
SUB = 8
SHARED = 6
PICKS = 16
CHOICES = (4, 5, 6)
VMEM_BYTES = 16 * 1024 * 1024


def whole(space):
    return pl.BlockSpec(memory_space=space)


def vmem_call(body, outs, n_smem, n_vmem, scratch=(), name=None, n_any=0, out_space=pltpu.VMEM, keep=True):
    call = pl.pallas_call(
        body,
        out_shape=outs,
        in_specs=[whole(pltpu.SMEM)] * n_smem + [whole(pl.ANY)] * n_any + [whole(pltpu.VMEM)] * n_vmem,
        out_specs=jax.tree.map(lambda _: whole(out_space), outs),
        scratch_shapes=list(scratch),
        compiler_params=pltpu.CompilerParams(vmem_limit_bytes=VMEM_BYTES),
        name=name,
    )

    def run(*args):
        if not keep:
            return call(*args)
        kept = [pltpu.with_memory_space_constraint(x, pltpu.VMEM) for x in args[n_smem + n_any :]]
        return call(*args[: n_smem + n_any], *kept)

    return run


def inverse_norm(wide):
    return lax.rsqrt(jnp.sum(wide * wide, axis=1, keepdims=True) + EPSILON)


def from_pieces(pieces, slot):
    row_tiles, col_tiles = pieces.shape[:2]
    return jnp.concatenate(
        [pieces[:, ct, slot].reshape(row_tiles * SUB, LANES) for ct in range(col_tiles)], axis=1
    )


def dot_nt(a, b):
    return lax.dot_general(a, b, (((1,), (1,)), ((), ())), preferred_element_type=jnp.float32)


def dot_tn(a, b):
    return lax.dot_general(a, b, (((0,), (0,)), ((), ())), preferred_element_type=jnp.float32)


def dot_nn(a, b):
    return lax.dot_general(a, b, (((1,), (0,)), ((), ())), preferred_element_type=jnp.float32)


def own_kernel(q_ref, d_ref, qu_ref, du_ref, inv_ref, et_ref):
    q_wide = q_ref[...].astype(jnp.float32)
    d_wide = d_ref[...].astype(jnp.float32)
    q_inv = inverse_norm(q_wide)
    d_inv = inverse_norm(d_wide)
    q = (q_wide * q_inv).astype(jnp.bfloat16)
    d = (d_wide * d_inv).astype(jnp.bfloat16)
    qu_ref[...] = q
    du_ref[...] = d
    lane = lax.broadcasted_iota(jnp.int32, inv_ref.shape, 1)
    inv_ref[...] = jnp.where(lane == 0, q_inv, d_inv)
    et_ref[...] = jnp.exp(LOGIT_SCALE * dot_nt(d, q))


def split_pair(value, odd):
    high = value.astype(jnp.bfloat16).astype(jnp.float32)
    return jnp.where(odd, value - high, high)


def tiles_kernel(qu_ref, et_own_ref, fetched_ref, send_ref, et_ref, row_ref, dk_ref):
    row_tiles, col_tiles = send_ref.shape[:2]
    q = qu_ref[...]
    pieces = fetched_ref[:, 0 : 2 * SUB, :].astype(jnp.float32)
    pieces = pieces.reshape(row_tiles, col_tiles, 2, SUB, LANES)
    et_own = et_own_ref[...]
    row_total = jnp.sum(et_own, axis=0, keepdims=True)
    col_own = jnp.sum(et_own, axis=1, keepdims=True)
    ets, cols = [], []
    for k in range(2):
        wide = from_pieces(pieces, k)
        unit = (wide * inverse_norm(wide)).astype(jnp.bfloat16)
        dk_ref[k] = unit
        et = jnp.exp(LOGIT_SCALE * dot_nt(unit, q))
        et_ref[k] = et
        row_total = row_total + jnp.sum(et, axis=0, keepdims=True)
        cols.append(jnp.sum(et, axis=1, keepdims=True))
        ets.append(et)
    row_ref[...] = row_total
    row_inv = 1.0 / row_total
    half = 0.5 * LOGIT_SCALE
    parts = []
    for make in (lambda e: e * row_inv, lambda e: e):
        parts.append([half * dot_nn(make(e).astype(jnp.bfloat16), q) for e in ets])
    for ct in range(col_tiles):
        lanes = slice(ct * LANES, (ct + 1) * LANES)
        for kind in range(2):
            pair = [x[:, lanes].reshape(row_tiles, 1, SUB, LANES) for x in parts[kind]]
            both = jnp.concatenate(pair, axis=1).reshape(row_tiles, 2 * SUB, LANES)
            send_ref[:, ct, 2 * SUB * kind : 2 * SUB * (kind + 1), :] = both.astype(jnp.bfloat16)
    rows = row_tiles * SUB
    lane = lax.broadcasted_iota(jnp.int32, (rows, LANES), 1)
    value = jnp.where(lane < 2, col_own, jnp.where(lane < 4, cols[0], cols[1]))
    scalars = split_pair(value, lane % 2 == 1).reshape(row_tiles, SUB, LANES).astype(jnp.bfloat16)
    for ct in range(col_tiles):
        send_ref[:, ct, 4 * SUB :, :] = scalars


def combine_kernel(cols_ref, recv_ref, out_ref, acc_a, acc_b, acc_t):
    blocks = recv_ref.shape[0]
    acc_a[...] = jnp.zeros_like(acc_a)
    acc_b[...] = jnp.zeros_like(acc_b)
    lane3 = lax.broadcasted_iota(jnp.int32, acc_t.shape, 2)
    own = recv_ref[:, 4 * SUB :, :].astype(jnp.float32)
    acc_t[...] = jnp.where(lane3 < 2, own, 0.0)
    lane = lax.broadcasted_iota(jnp.int32, (SUB, LANES), 1)
    masks = [(lane >= 2) & (lane < 4), (lane >= 4) & (lane < 6)]

    def add(source, carry):
        a = recv_ref[source, 0 : 2 * SUB, :].astype(jnp.float32)
        b = recv_ref[source, 2 * SUB : 4 * SUB, :].astype(jnp.float32)
        t = recv_ref[source, 4 * SUB :, :].astype(jnp.float32)
        for k in range(2):
            col = cols_ref[2 * source + k]
            acc_a[col] = acc_a[col] + a[k * SUB : (k + 1) * SUB]
            acc_b[col] = acc_b[col] + b[k * SUB : (k + 1) * SUB]
            acc_t[col] = acc_t[col] + jnp.where(masks[k], t, 0.0)
        return carry

    lax.fori_loop(0, blocks, add, 0, unroll=8)
    total = jnp.broadcast_to(jnp.sum(acc_t[...], axis=2, keepdims=True), acc_t.shape)
    acc_t[...] = total
    acc_a[...] = acc_a[...] + acc_b[...] / total
    odd = lane % 2 == 1

    def emit(dest, carry):
        value = jnp.where(
            lane < 2,
            acc_t[dest],
            jnp.where(lane < 4, acc_t[cols_ref[2 * dest]], acc_t[cols_ref[2 * dest + 1]]),
        )
        both = jnp.concatenate([acc_a[dest], split_pair(value, odd)], axis=0)
        out_ref[dest] = both.astype(jnp.bfloat16)
        return carry

    lax.fori_loop(0, blocks, emit, 0, unroll=8)


def unit_grad(wide, inverse, upstream):
    radial = jnp.sum(wide * upstream, axis=1, keepdims=True)
    return upstream * inverse - wide * (radial * inverse * inverse * inverse)


def final_kernel(
    q_ref, d_ref, qu_ref, du_ref, inv_ref, et_own_ref, et_ref, row_ref, dk_ref, home_ref, gq_ref, gd_ref
):
    rows, features = q_ref.shape
    row_tiles, col_tiles = rows // SUB, features // LANES
    pieces = home_ref[...].astype(jnp.float32).reshape(row_tiles, col_tiles, 2, SUB, LANES)
    scalars = pieces[:, 0, 1].reshape(rows, LANES)
    totals = [scalars[:, 2 * i : 2 * i + 1] + scalars[:, 2 * i + 1 : 2 * i + 2] for i in range(3)]
    row_inv = 1.0 / row_ref[...]

    def weight(et, total):
        return 0.5 * (et * row_inv + et * (1.0 / total))

    own = weight(et_own_ref[...], totals[0])
    diagonal = lax.broadcasted_iota(jnp.int32, own.shape, 0) == lax.broadcasted_iota(
        jnp.int32, own.shape, 1
    )
    own = (own - jnp.where(diagonal, 1.0, 0.0)).astype(jnp.bfloat16)

    def part(x):
        return (LOGIT_SCALE * x).astype(jnp.bfloat16).astype(jnp.float32)

    query = part(dot_tn(own, du_ref[...]))
    for k in range(2):
        w = weight(et_ref[k], totals[k + 1]).astype(jnp.bfloat16)
        query = query + part(dot_tn(w, dk_ref[k]))
    gq_ref[...] = unit_grad(q_ref[...].astype(jnp.float32), inv_ref[:, 0:1], query)
    doc = part(dot_nn(own, qu_ref[...])) + from_pieces(pieces, 0)
    gd_ref[...] = unit_grad(d_ref[...].astype(jnp.float32), inv_ref[:, 1:2], doc)


def first_gather_kernel(cols_any, spread_ref, query_ref, out_ref, cols_ref, sem):
    bring = pltpu.make_async_copy(cols_any, cols_ref, sem)
    bring.start()
    out_ref[:, 2 * SUB :, :] = query_ref[...]
    bring.wait()

    def step(dest, carry):
        tiles = [spread_ref[cols_ref[2 * dest + k]] for k in range(2)]
        for slot, tile in enumerate(tiles):
            out_ref[dest, slot * SUB : (slot + 1) * SUB, :] = tile
        return carry

    lax.fori_loop(0, out_ref.shape[0], step, 0, unroll=16)


def eye_mask(n):
    return lax.broadcasted_iota(jnp.int32, (n, n), 0) == lax.broadcasted_iota(jnp.int32, (n, n), 1)


def to_lanes(column, eye):
    return jnp.sum(jnp.where(eye, column, 0.0), axis=0, keepdims=True)


def to_sublanes(row, eye):
    return jnp.sum(jnp.where(eye, row, 0.0), axis=1, keepdims=True)


def own_pair_kernel(q_ref, d_ref, qu_ref, du_ref, inv_ref, e_ref, et_ref):
    own_kernel(q_ref, d_ref, qu_ref, du_ref, inv_ref, et_ref)
    e_ref[...] = jnp.exp(LOGIT_SCALE * dot_nt(qu_ref[...], du_ref[...]))


def fetched_rows(fetched_ref, slot, row_tiles, col_tiles):
    piece = fetched_ref[:, slot * SUB : (slot + 1) * SUB, :].astype(jnp.float32)
    return from_pieces(piece.reshape(row_tiles, col_tiles, 1, SUB, LANES), 0)


def row_side_kernel(
    table_any, qu_ref, du_ref, e_own_ref, et_own_ref, fetched_ref,
    send_ref, e_ref, row_ref, units_ref, extra_ref, table_ref, sem
):
    bring = pltpu.make_async_copy(table_any, table_ref, sem)
    bring.start()
    rows, features = qu_ref.shape
    row_tiles, col_tiles = rows // SUB, features // LANES
    shared = send_ref.shape[1] // SUB - 1
    stride = table_ref.shape[0] // send_ref.shape[0]
    eye = eye_mask(rows)
    q = qu_ref[...]
    units_ref[0:rows] = du_ref[...]
    row_total = jnp.sum(e_own_ref[...], axis=1, keepdims=True)
    columns = [to_lanes(jnp.sum(et_own_ref[...], axis=1, keepdims=True), eye)]
    for k in range(2):
        piece = fetched_ref[...].reshape(row_tiles, col_tiles, 3, SUB, LANES)[:, :, k : k + 1]
        wide = from_pieces(piece.astype(jnp.float32), 0)
        unit = (wide * inverse_norm(wide)).astype(jnp.bfloat16)
        units_ref[(k + 1) * rows : (k + 2) * rows] = unit
        e = jnp.exp(LOGIT_SCALE * dot_nt(q, unit))
        e_ref[k] = e
        row_total = row_total + jnp.sum(e, axis=1, keepdims=True)
        columns.append(jnp.sum(e, axis=0, keepdims=True))
    row_ref[...] = row_total
    doubled = []
    for x in [to_lanes(row_total, eye)] + columns:
        high = x.astype(jnp.bfloat16).astype(jnp.float32)
        doubled += [high, x - high]
    extra_ref[...] = jnp.concatenate(doubled, axis=0).astype(jnp.bfloat16)
    send_ref[:, shared * SUB :, :] = jnp.broadcast_to(extra_ref[...][None], (send_ref.shape[0], SUB, LANES))

    bring.wait()

    def step(dest, carry):
        tiles = [fetched_ref[table_ref[dest * stride + slot]] for slot in range(shared)]
        for slot, tile in enumerate(tiles):
            send_ref[dest, slot * SUB : (slot + 1) * SUB, :] = tile
        return carry

    lax.fori_loop(0, send_ref.shape[0], step, 0, unroll=4)


def doc_side_kernel(
    info_any, other_any, pick_ref, qu_ref, du_ref, et_own_ref, recv_ref,
    acc_ref, partner_ref, sums_ref, units_ref, pair_ref, sem, info_ref, info_sem
):
    bring = pltpu.make_async_copy(other_any, pair_ref.at[1], sem)
    bring.start()
    bring_info = pltpu.make_async_copy(info_any, info_ref, info_sem)
    bring_info.start()
    rows, features = qu_ref.shape
    row_tiles, col_tiles = rows // SUB, features // LANES
    blocks = recv_ref.shape[0]
    shared = recv_ref.shape[1] // SUB - 1
    eye = eye_mask(rows)
    messages = recv_ref[:, shared * SUB :, :].astype(jnp.float32).reshape(blocks * SUB, LANES)
    sums = dot_nn(pick_ref[...], messages.astype(jnp.bfloat16))
    sums_ref[...] = sums
    inverse = [1.0 / to_sublanes(sums[i : i + 1], eye) for i in range(2)]

    def weight(et, row_total, col_inverse):
        return 0.5 * (et * (1.0 / row_total) + et * col_inverse)

    q = qu_ref[...]
    own = weight(et_own_ref[...], sums[4:5], inverse[0]) - jnp.where(eye, 1.0, 0.0)
    units_ref[0:rows] = q
    pair_ref[0] = du_ref[...]
    weights = [[own.astype(jnp.bfloat16)], [jnp.zeros((rows, rows), jnp.bfloat16)]]
    bring.wait()
    bring_info.wait()
    for slot in range(shared):
        entry = info_ref[slot]
        side = 1 - lax.rem(entry, 2)
        unit = fetched_rows(recv_ref, slot, row_tiles, col_tiles).astype(jnp.bfloat16)
        units_ref[(slot + 1) * rows : (slot + 2) * rows] = unit
        docs = pair_ref[side]
        et = jnp.exp(LOGIT_SCALE * dot_nt(docs, unit))
        live = entry > 0
        total = jnp.where(live, sums[5 + slot : 6 + slot], 1.0)
        w = weight(et, total, jnp.where(side == 1, inverse[1], inverse[0]))
        for i in range(2):
            weights[i].append(jnp.where(live & (side == i), w, 0.0).astype(jnp.bfloat16))
    weights = jnp.concatenate([jnp.concatenate(w, axis=1) for w in weights], axis=0)
    grads = LOGIT_SCALE * dot_nn(weights, units_ref[...])
    acc_ref[...] = grads[0:rows]
    partner_ref[...] = grads[rows:].astype(jnp.bfloat16)


def query_side_kernel(sums_ref, q_ref, inv_ref, e_own_ref, e_ref, row_ref, units_ref, gq_ref, buf, sems):
    eye = eye_mask(q_ref.shape[0])
    row_inv = 1.0 / row_ref[...]

    def weight(e, which):
        return 0.5 * (e * row_inv + e * (1.0 / sums_ref[which : which + 1, :]))

    weights = [weight(e_own_ref[...], 0) - jnp.where(eye, 1.0, 0.0)]
    weights += [weight(e_ref[k], 2 + k) for k in range(2)]
    query = LOGIT_SCALE * dot_nn(jnp.concatenate(weights, axis=1).astype(jnp.bfloat16), units_ref[...])
    write_grad(gq_ref, buf, sems, lambda some: (q_ref[some], inv_ref[some, 0:1], query[some]))


def write_grad(out_ref, buf, sems, rows_of):
    parts = sems.shape[0]
    step = buf.shape[0] // parts
    copies = []
    for j in range(parts):
        some = slice(j * step, (j + 1) * step)
        raw, inverse, upstream = rows_of(some)
        buf[some] = unit_grad(raw.astype(jnp.float32), inverse, upstream)
        at = pl.ds(j * step, step)
        copies.append(pltpu.make_async_copy(buf.at[at], out_ref.at[at], sems.at[j]))
        copies[-1].start()
    for copy in copies:
        copy.wait()


def doc_final_kernel(d_ref, inv_ref, acc_ref, swapped_ref, gd_ref, buf, sems):
    def rows_of(some):
        return d_ref[some], inv_ref[some, 1:2], acc_ref[some] + swapped_ref[some].astype(jnp.float32)

    write_grad(gd_ref, buf, sems, rows_of)


def exchange(x):
    return lax.all_to_all(x, "dp", split_axis=0, concat_axis=0, tiled=True)


def row_columns(pair_blocks, active_pair_count, blocks):
    slots = pair_blocks.shape[1]
    live = jnp.arange(slots)[None, :] < active_pair_count[:, None]
    rows = jnp.where(live, pair_blocks[:, :, 0], -1).reshape(1, -1)
    cols = pair_blocks[:, :, 1].reshape(1, -1)
    match = rows == jnp.arange(blocks)[:, None]
    low = jnp.min(jnp.where(match, cols, blocks - 1), axis=1)
    high = jnp.max(jnp.where(match, cols, 0), axis=1)
    return jnp.stack([low, high], axis=1).reshape(-1).astype(jnp.int32)


def shared_slots(cols, blocks):
    tiles = jnp.arange(cols.shape[0])
    chip = cols // 2
    before = (chip[:, None] == chip[None, :]) & (tiles[None, :] < tiles[:, None])
    rank = jnp.sum(before.astype(jnp.int32), axis=1)
    device = 2 * chip + rank % 2
    slot = rank // 2
    entry = 1 + 2 * (tiles // 2) + (cols % 2 != rank % 2).astype(jnp.int32)
    place = device * SHARED + slot
    hit = (place[None, :] == jnp.arange(blocks * SHARED)[:, None]) & (slot[None, :] < SHARED)
    table = jnp.sum(jnp.where(hit, entry[None, :], 0), axis=1).astype(jnp.int32)
    level = sum((rank >= 2 * shared).astype(jnp.int32) for shared in CHOICES)
    return table.reshape(blocks, SHARED), jnp.max(level)


def message_picks(cols, mine, me, blocks):
    source = jnp.arange(blocks * SUB) // SUB
    kind = (jnp.arange(blocks * SUB) % SUB) // 2
    pair = cols.reshape(blocks, 2)
    own_pair = lax.dynamic_index_in_dim(pair, me, 0, keepdims=False)
    columns = jnp.concatenate([jnp.stack([me, me ^ 1]).astype(jnp.int32), own_pair])[:, None]
    first = jnp.repeat(pair[:, 0], SUB)
    second = jnp.repeat(pair[:, 1], SUB)
    named = jnp.where(kind == 1, source, jnp.where(kind == 2, first, second))
    column_hit = (named[None, :] == columns) & (kind > 0)[None, :]
    row_blocks = jnp.concatenate([me.reshape(1).astype(jnp.int32), (mine + 1) // 2 - 1])[:, None]
    row_hit = (source[None, :] == row_blocks) & (kind == 0)[None, :]
    hits = jnp.concatenate([column_hit, row_hit], axis=0).astype(jnp.bfloat16)
    return jnp.pad(hits, ((0, PICKS - hits.shape[0]), (0, 0)))


def pieces(x):
    rows, features = x.shape
    tiled = x.reshape(rows // SUB, SUB, features // LANES, LANES).transpose(0, 2, 1, 3)
    return tiled.reshape(-1, SUB, LANES)


def small_table(x):
    return pltpu.SMEM(x.shape, x.dtype), pltpu.SemaphoreType.DMA


def fetch(cols, spread, query_unit):
    blocks = lax.axis_size("dp")
    wanted = vmem_call(
        first_gather_kernel,
        pltpu.VMEM((blocks, 3 * SUB, LANES), jnp.bfloat16),
        0,
        2,
        small_table(cols),
        name="gather",
        n_any=1,
    )(cols, spread, pieces(query_unit))
    return exchange(wanted)


def general_path(query_emb, doc_emb, spread, cols, table, info, picks, own):
    qu, du, inv, _, et_own, _ = own
    fetched = fetch(cols, spread, qu)
    blocks = lax.axis_size("dp")
    rows, features = query_emb.shape
    row_tiles, col_tiles = rows // SUB, features // LANES
    sds = pltpu.VMEM
    bf16, f32 = jnp.bfloat16, jnp.float32
    send, et, row_total, dk = vmem_call(
        tiles_kernel,
        (
            sds((row_tiles, col_tiles, 5 * SUB, LANES), bf16),
            sds((2, rows, rows), f32),
            sds((1, rows), f32),
            sds((2, rows, features), bf16),
        ),
        0,
        3,
        name="tiles",
    )(qu, et_own, fetched)
    parts = exchange(send.reshape(blocks, 5 * SUB, LANES))
    acc = pltpu.VMEM((blocks, SUB, LANES), f32)
    combined = vmem_call(
        combine_kernel, sds((blocks, 2 * SUB, LANES), bf16), 1, 1, (acc, acc, acc), name="combine"
    )(cols, parts)
    home = exchange(combined)
    grad = jax.ShapeDtypeStruct((rows, features), f32)
    return vmem_call(final_kernel, (grad, grad), 0, 10, name="final")(
        query_emb, doc_emb, qu, du, inv, et_own, et, row_total, dk, home
    )


def short_path(shared, query_emb, doc_emb, spread, cols, table, info, picks, own):
    qu, du, inv, e_own, et_own, other = own
    fetched = fetch(cols, spread, qu)
    blocks = lax.axis_size("dp")
    rows, features = query_emb.shape
    assert rows == LANES
    sds = pltpu.VMEM
    bf16, f32 = jnp.bfloat16, jnp.float32
    wide = sds((rows, features), bf16)
    grad = jax.ShapeDtypeStruct((rows, features), f32)
    send, e, row_total, doc_units = vmem_call(
        row_side_kernel,
        (
            sds((blocks, (shared + 1) * SUB, LANES), bf16),
            sds((2, rows, rows), f32),
            sds((rows, 1), f32),
            sds((3 * rows, features), bf16),
        ),
        0,
        5,
        (pltpu.VMEM((SUB, LANES), bf16), *small_table(table)),
        name="rows",
        n_any=1,
    )(table, qu, du, e_own, et_own, fetched.reshape(3 * blocks, SUB, LANES))
    recv = exchange(send)
    acc, partner, sums = vmem_call(
        doc_side_kernel,
        (sds((rows, features), f32), wide, sds((PICKS, LANES), f32)),
        0,
        5,
        (
            pltpu.VMEM(((shared + 1) * rows, features), bf16),
            pltpu.VMEM((2, rows, features), bf16),
            pltpu.SemaphoreType.DMA,
            *small_table(info),
        ),
        name="docs",
        n_any=2,
    )(info, other, picks, qu, du, et_own, recv)
    swapped = swap_cores(partner)
    grad_scratch = (pltpu.VMEM((rows, features), f32), pltpu.SemaphoreType.DMA((4,)))
    grad_query = vmem_call(
        query_side_kernel, grad, 0, 7, grad_scratch, name="queries", out_space=pl.ANY
    )(sums, query_emb, inv, e_own, e, row_total, doc_units)
    grad_doc = vmem_call(
        doc_final_kernel, grad, 0, 4, grad_scratch, name="final", out_space=pl.ANY
    )(doc_emb, inv, acc, swapped)
    return grad_query, grad_doc


def swap_cores(x):
    return lax.ppermute(x, "dp", [(i, i ^ 1) for i in range(lax.axis_size("dp"))])


def on_device(query_emb, doc_emb, pair_blocks, active_pair_count):
    blocks = lax.axis_size("dp")
    me = lax.axis_index("dp")
    rows, features = query_emb.shape
    row_tiles, col_tiles = rows // SUB, features // LANES
    assert row_tiles * col_tiles == blocks

    spread = exchange(pieces(doc_emb))
    cols = row_columns(pair_blocks, active_pair_count, blocks)
    mat, wide = pltpu.VMEM((rows, rows), jnp.float32), pltpu.VMEM((rows, features), jnp.bfloat16)
    own = vmem_call(
        own_pair_kernel, (wide, wide, pltpu.VMEM((rows, 2), jnp.float32), mat, mat), 0, 2, name="own", keep=False
    )(query_emb, doc_emb)
    own = (*own, swap_cores(own[1]))
    table, choice = shared_slots(cols, blocks)
    info = lax.dynamic_index_in_dim(table, me, 0, keepdims=False)
    picks = message_picks(cols, info, me, blocks)
    table = jnp.pad(3 * (jnp.maximum(table - 1, 0) // 2) + 2, ((0, 0), (0, SUB - SHARED))).reshape(-1)
    info = jnp.pad(info, (0, LANES - SHARED))
    spread, cols, table, info, picks, choice, own = lax.optimization_barrier(
        (spread, cols, table, info, picks, choice, own)
    )
    args = (query_emb, doc_emb, spread, cols, table, info, picks, own)
    paths = [functools.partial(short_path, shared) for shared in CHOICES] + [general_path]
    return lax.switch(choice, paths, *args)


def solution(mesh):
    return jax.shard_map(
        on_device,
        mesh=mesh,
        in_specs=(P("dp", None), P("dp", None), P(), P()),
        out_specs=(P("dp", None), P("dp", None)),
        check_vma=False,
    )
```

```python
import functools

import jax
import jax.numpy as jnp
from jax import lax
from jax.experimental import pallas as pl
from jax.experimental.pallas import tpu as pltpu
from jax.sharding import PartitionSpec as P

LOGIT_SCALE = 64.0
EPSILON = 1e-06
LANES = 128
SUB = 8
SHARED = 6
PICKS = 16
CHOICES = (4, 5, 6)
VMEM_BYTES = 16 * 1024 * 1024


def whole(space):
    return pl.BlockSpec(memory_space=space)


def vmem_call(body, outs, n_smem, n_vmem, scratch=(), name=None, n_any=0, out_space=pltpu.VMEM, keep=True):
    call = pl.pallas_call(
        body,
        out_shape=outs,
        in_specs=[whole(pltpu.SMEM)] * n_smem + [whole(pl.ANY)] * n_any + [whole(pltpu.VMEM)] * n_vmem,
        out_specs=jax.tree.map(lambda _: whole(out_space), outs),
        scratch_shapes=list(scratch),
        compiler_params=pltpu.CompilerParams(vmem_limit_bytes=VMEM_BYTES),
        name=name,
    )

    def run(*args):
        if not keep:
            return call(*args)
        kept = [pltpu.with_memory_space_constraint(x, pltpu.VMEM) for x in args[n_smem + n_any :]]
        return call(*args[: n_smem + n_any], *kept)

    return run


def inverse_norm(wide):
    return lax.rsqrt(jnp.sum(wide * wide, axis=1, keepdims=True) + EPSILON)


def from_pieces(pieces, slot):
    row_tiles, col_tiles = pieces.shape[:2]
    return jnp.concatenate(
        [pieces[:, ct, slot].reshape(row_tiles * SUB, LANES) for ct in range(col_tiles)], axis=1
    )


def dot_nt(a, b):
    return lax.dot_general(a, b, (((1,), (1,)), ((), ())), preferred_element_type=jnp.float32)


def dot_tn(a, b):
    return lax.dot_general(a, b, (((0,), (0,)), ((), ())), preferred_element_type=jnp.float32)


def dot_nn(a, b):
    return lax.dot_general(a, b, (((1,), (0,)), ((), ())), preferred_element_type=jnp.float32)


def own_kernel(q_ref, d_ref, qu_ref, du_ref, inv_ref, et_ref):
    q_wide = q_ref[...].astype(jnp.float32)
    d_wide = d_ref[...].astype(jnp.float32)
    q_inv = inverse_norm(q_wide)
    d_inv = inverse_norm(d_wide)
    q = (q_wide * q_inv).astype(jnp.bfloat16)
    d = (d_wide * d_inv).astype(jnp.bfloat16)
    qu_ref[...] = q
    du_ref[...] = d
    lane = lax.broadcasted_iota(jnp.int32, inv_ref.shape, 1)
    inv_ref[...] = jnp.where(lane == 0, q_inv, d_inv)
    et_ref[...] = jnp.exp(LOGIT_SCALE * dot_nt(d, q))


def split_pair(value, odd):
    high = value.astype(jnp.bfloat16).astype(jnp.float32)
    return jnp.where(odd, value - high, high)


def tiles_kernel(qu_ref, et_own_ref, fetched_ref, send_ref, et_ref, row_ref, dk_ref):
    row_tiles, col_tiles = send_ref.shape[:2]
    q = qu_ref[...]
    pieces = fetched_ref[:, 0 : 2 * SUB, :].astype(jnp.float32)
    pieces = pieces.reshape(row_tiles, col_tiles, 2, SUB, LANES)
    et_own = et_own_ref[...]
    row_total = jnp.sum(et_own, axis=0, keepdims=True)
    col_own = jnp.sum(et_own, axis=1, keepdims=True)
    ets, cols = [], []
    for k in range(2):
        wide = from_pieces(pieces, k)
        unit = (wide * inverse_norm(wide)).astype(jnp.bfloat16)
        dk_ref[k] = unit
        et = jnp.exp(LOGIT_SCALE * dot_nt(unit, q))
        et_ref[k] = et
        row_total = row_total + jnp.sum(et, axis=0, keepdims=True)
        cols.append(jnp.sum(et, axis=1, keepdims=True))
        ets.append(et)
    row_ref[...] = row_total
    row_inv = 1.0 / row_total
    half = 0.5 * LOGIT_SCALE
    parts = []
    for make in (lambda e: e * row_inv, lambda e: e):
        parts.append([half * dot_nn(make(e).astype(jnp.bfloat16), q) for e in ets])
    for ct in range(col_tiles):
        lanes = slice(ct * LANES, (ct + 1) * LANES)
        for kind in range(2):
            pair = [x[:, lanes].reshape(row_tiles, 1, SUB, LANES) for x in parts[kind]]
            both = jnp.concatenate(pair, axis=1).reshape(row_tiles, 2 * SUB, LANES)
            send_ref[:, ct, 2 * SUB * kind : 2 * SUB * (kind + 1), :] = both.astype(jnp.bfloat16)
    rows = row_tiles * SUB
    lane = lax.broadcasted_iota(jnp.int32, (rows, LANES), 1)
    value = jnp.where(lane < 2, col_own, jnp.where(lane < 4, cols[0], cols[1]))
    scalars = split_pair(value, lane % 2 == 1).reshape(row_tiles, SUB, LANES).astype(jnp.bfloat16)
    for ct in range(col_tiles):
        send_ref[:, ct, 4 * SUB :, :] = scalars


def combine_kernel(cols_ref, recv_ref, out_ref, acc_a, acc_b, acc_t):
    blocks = recv_ref.shape[0]
    acc_a[...] = jnp.zeros_like(acc_a)
    acc_b[...] = jnp.zeros_like(acc_b)
    lane3 = lax.broadcasted_iota(jnp.int32, acc_t.shape, 2)
    own = recv_ref[:, 4 * SUB :, :].astype(jnp.float32)
    acc_t[...] = jnp.where(lane3 < 2, own, 0.0)
    lane = lax.broadcasted_iota(jnp.int32, (SUB, LANES), 1)
    masks = [(lane >= 2) & (lane < 4), (lane >= 4) & (lane < 6)]

    def add(source, carry):
        a = recv_ref[source, 0 : 2 * SUB, :].astype(jnp.float32)
        b = recv_ref[source, 2 * SUB : 4 * SUB, :].astype(jnp.float32)
        t = recv_ref[source, 4 * SUB :, :].astype(jnp.float32)
        for k in range(2):
            col = cols_ref[2 * source + k]
            acc_a[col] = acc_a[col] + a[k * SUB : (k + 1) * SUB]
            acc_b[col] = acc_b[col] + b[k * SUB : (k + 1) * SUB]
            acc_t[col] = acc_t[col] + jnp.where(masks[k], t, 0.0)
        return carry

    lax.fori_loop(0, blocks, add, 0, unroll=8)
    total = jnp.broadcast_to(jnp.sum(acc_t[...], axis=2, keepdims=True), acc_t.shape)
    acc_t[...] = total
    acc_a[...] = acc_a[...] + acc_b[...] / total
    odd = lane % 2 == 1

    def emit(dest, carry):
        value = jnp.where(
            lane < 2,
            acc_t[dest],
            jnp.where(lane < 4, acc_t[cols_ref[2 * dest]], acc_t[cols_ref[2 * dest + 1]]),
        )
        both = jnp.concatenate([acc_a[dest], split_pair(value, odd)], axis=0)
        out_ref[dest] = both.astype(jnp.bfloat16)
        return carry

    lax.fori_loop(0, blocks, emit, 0, unroll=8)


def unit_grad(wide, inverse, upstream):
    radial = jnp.sum(wide * upstream, axis=1, keepdims=True)
    return upstream * inverse - wide * (radial * inverse * inverse * inverse)


def final_kernel(
    q_ref, d_ref, qu_ref, du_ref, inv_ref, et_own_ref, et_ref, row_ref, dk_ref, home_ref, gq_ref, gd_ref
):
    rows, features = q_ref.shape
    row_tiles, col_tiles = rows // SUB, features // LANES
    pieces = home_ref[...].astype(jnp.float32).reshape(row_tiles, col_tiles, 2, SUB, LANES)
    scalars = pieces[:, 0, 1].reshape(rows, LANES)
    totals = [scalars[:, 2 * i : 2 * i + 1] + scalars[:, 2 * i + 1 : 2 * i + 2] for i in range(3)]
    row_inv = 1.0 / row_ref[...]

    def weight(et, total):
        return 0.5 * (et * row_inv + et * (1.0 / total))

    own = weight(et_own_ref[...], totals[0])
    diagonal = lax.broadcasted_iota(jnp.int32, own.shape, 0) == lax.broadcasted_iota(
        jnp.int32, own.shape, 1
    )
    own = (own - jnp.where(diagonal, 1.0, 0.0)).astype(jnp.bfloat16)

    def part(x):
        return (LOGIT_SCALE * x).astype(jnp.bfloat16).astype(jnp.float32)

    query = part(dot_tn(own, du_ref[...]))
    for k in range(2):
        w = weight(et_ref[k], totals[k + 1]).astype(jnp.bfloat16)
        query = query + part(dot_tn(w, dk_ref[k]))
    gq_ref[...] = unit_grad(q_ref[...].astype(jnp.float32), inv_ref[:, 0:1], query)
    doc = part(dot_nn(own, qu_ref[...])) + from_pieces(pieces, 0)
    gd_ref[...] = unit_grad(d_ref[...].astype(jnp.float32), inv_ref[:, 1:2], doc)


def first_gather_kernel(cols_any, spread_ref, query_ref, out_ref, cols_ref, sem):
    bring = pltpu.make_async_copy(cols_any, cols_ref, sem)
    bring.start()
    out_ref[:, 2 * SUB :, :] = query_ref[...]
    bring.wait()

    def step(dest, carry):
        tiles = [spread_ref[cols_ref[2 * dest + k]] for k in range(2)]
        for slot, tile in enumerate(tiles):
            out_ref[dest, slot * SUB : (slot + 1) * SUB, :] = tile
        return carry

    lax.fori_loop(0, out_ref.shape[0], step, 0, unroll=16)


def eye_mask(n):
    return lax.broadcasted_iota(jnp.int32, (n, n), 0) == lax.broadcasted_iota(jnp.int32, (n, n), 1)


def to_lanes(column, eye):
    return jnp.sum(jnp.where(eye, column, 0.0), axis=0, keepdims=True)


def to_sublanes(row, eye):
    return jnp.sum(jnp.where(eye, row, 0.0), axis=1, keepdims=True)


def own_pair_kernel(q_ref, d_ref, qu_ref, du_ref, inv_ref, e_ref, et_ref):
    own_kernel(q_ref, d_ref, qu_ref, du_ref, inv_ref, et_ref)
    e_ref[...] = jnp.exp(LOGIT_SCALE * dot_nt(qu_ref[...], du_ref[...]))


def fetched_rows(fetched_ref, slot, row_tiles, col_tiles):
    piece = fetched_ref[:, slot * SUB : (slot + 1) * SUB, :].astype(jnp.float32)
    return from_pieces(piece.reshape(row_tiles, col_tiles, 1, SUB, LANES), 0)


def row_side_kernel(
    table_any, qu_ref, du_ref, e_own_ref, et_own_ref, fetched_ref,
    send_ref, e_ref, row_ref, units_ref, extra_ref, table_ref, sem
):
    bring = pltpu.make_async_copy(table_any, table_ref, sem)
    bring.start()
    rows, features = qu_ref.shape
    row_tiles, col_tiles = rows // SUB, features // LANES
    shared = send_ref.shape[1] // SUB - 1
    stride = table_ref.shape[0] // send_ref.shape[0]
    eye = eye_mask(rows)
    q = qu_ref[...]
    units_ref[0:rows] = du_ref[...]
    row_total = jnp.sum(e_own_ref[...], axis=1, keepdims=True)
    columns = [to_lanes(jnp.sum(et_own_ref[...], axis=1, keepdims=True), eye)]
    for k in range(2):
        piece = fetched_ref[...].reshape(row_tiles, col_tiles, 3, SUB, LANES)[:, :, k : k + 1]
        wide = from_pieces(piece.astype(jnp.float32), 0)
        unit = (wide * inverse_norm(wide)).astype(jnp.bfloat16)
        units_ref[(k + 1) * rows : (k + 2) * rows] = unit
        e = jnp.exp(LOGIT_SCALE * dot_nt(q, unit))
        e_ref[k] = e
        row_total = row_total + jnp.sum(e, axis=1, keepdims=True)
        columns.append(jnp.sum(e, axis=0, keepdims=True))
    row_ref[...] = row_total
    doubled = []
    for x in [to_lanes(row_total, eye)] + columns:
        high = x.astype(jnp.bfloat16).astype(jnp.float32)
        doubled += [high, x - high]
    extra_ref[...] = jnp.concatenate(doubled, axis=0).astype(jnp.bfloat16)
    send_ref[:, shared * SUB :, :] = jnp.broadcast_to(extra_ref[...][None], (send_ref.shape[0], SUB, LANES))

    bring.wait()

    def step(dest, carry):
        tiles = [fetched_ref[table_ref[dest * stride + slot]] for slot in range(shared)]
        for slot, tile in enumerate(tiles):
            send_ref[dest, slot * SUB : (slot + 1) * SUB, :] = tile
        return carry

    lax.fori_loop(0, send_ref.shape[0], step, 0, unroll=4)


def doc_side_kernel(
    info_any, other_any, pick_ref, qu_ref, du_ref, et_own_ref, recv_ref,
    acc_ref, partner_ref, sums_ref, units_ref, other_ref, sem, info_ref, info_sem
):
    bring = pltpu.make_async_copy(other_any, other_ref, sem)
    bring.start()
    bring_info = pltpu.make_async_copy(info_any, info_ref, info_sem)
    bring_info.start()
    rows, features = qu_ref.shape
    row_tiles, col_tiles = rows // SUB, features // LANES
    blocks = recv_ref.shape[0]
    shared = recv_ref.shape[1] // SUB - 1
    eye = eye_mask(rows)
    messages = recv_ref[:, shared * SUB :, :].astype(jnp.float32).reshape(blocks * SUB, LANES)
    sums = dot_nn(pick_ref[...], messages.astype(jnp.bfloat16))
    sums_ref[...] = sums
    inverse = [1.0 / to_sublanes(sums[i : i + 1], eye) for i in range(2)]

    def weight(et, row_total, col_inverse):
        return 0.5 * (et * (1.0 / row_total) + et * col_inverse)

    q = qu_ref[...]
    own = weight(et_own_ref[...], sums[4:5], inverse[0]) - jnp.where(eye, 1.0, 0.0)
    units_ref[0:rows] = q
    weights = [[own.astype(jnp.bfloat16)], [jnp.zeros((rows, rows), jnp.bfloat16)]]
    bring.wait()
    bring_info.wait()
    for slot in range(shared):
        entry = info_ref[slot]
        side = 1 - lax.rem(entry, 2)
        unit = fetched_rows(recv_ref, slot, row_tiles, col_tiles).astype(jnp.bfloat16)
        units_ref[(slot + 1) * rows : (slot + 2) * rows] = unit
        docs = jnp.where(side == 1, other_ref[...], du_ref[...])
        et = jnp.exp(LOGIT_SCALE * dot_nt(docs, unit))
        live = entry > 0
        total = jnp.where(live, sums[5 + slot : 6 + slot], 1.0)
        w = weight(et, total, jnp.where(side == 1, inverse[1], inverse[0]))
        for i in range(2):
            weights[i].append(jnp.where(live & (side == i), w, 0.0).astype(jnp.bfloat16))
    weights = jnp.concatenate([jnp.concatenate(w, axis=1) for w in weights], axis=0)
    grads = LOGIT_SCALE * dot_nn(weights, units_ref[...])
    acc_ref[...] = grads[0:rows]
    partner_ref[...] = grads[rows:].astype(jnp.bfloat16)


def query_side_kernel(sums_ref, q_ref, inv_ref, e_own_ref, e_ref, row_ref, units_ref, gq_ref, buf, sems):
    eye = eye_mask(q_ref.shape[0])
    row_inv = 1.0 / row_ref[...]

    def weight(e, which):
        return 0.5 * (e * row_inv + e * (1.0 / sums_ref[which : which + 1, :]))

    weights = [weight(e_own_ref[...], 0) - jnp.where(eye, 1.0, 0.0)]
    weights += [weight(e_ref[k], 2 + k) for k in range(2)]
    query = LOGIT_SCALE * dot_nn(jnp.concatenate(weights, axis=1).astype(jnp.bfloat16), units_ref[...])
    write_grad(gq_ref, buf, sems, lambda some: (q_ref[some], inv_ref[some, 0:1], query[some]))


def write_grad(out_ref, buf, sems, rows_of):
    parts = sems.shape[0]
    step = buf.shape[0] // parts
    copies = []
    for j in range(parts):
        some = slice(j * step, (j + 1) * step)
        raw, inverse, upstream = rows_of(some)
        buf[some] = unit_grad(raw.astype(jnp.float32), inverse, upstream)
        at = pl.ds(j * step, step)
        copies.append(pltpu.make_async_copy(buf.at[at], out_ref.at[at], sems.at[j]))
        copies[-1].start()
    for copy in copies:
        copy.wait()


def doc_final_kernel(d_ref, inv_ref, acc_ref, swapped_ref, gd_ref, buf, sems):
    def rows_of(some):
        return d_ref[some], inv_ref[some, 1:2], acc_ref[some] + swapped_ref[some].astype(jnp.float32)

    write_grad(gd_ref, buf, sems, rows_of)


def exchange(x):
    return lax.all_to_all(x, "dp", split_axis=0, concat_axis=0, tiled=True)


def row_columns(pair_blocks, active_pair_count, blocks):
    slots = pair_blocks.shape[1]
    live = jnp.arange(slots)[None, :] < active_pair_count[:, None]
    rows = jnp.where(live, pair_blocks[:, :, 0], -1).reshape(1, -1)
    cols = pair_blocks[:, :, 1].reshape(1, -1)
    match = rows == jnp.arange(blocks)[:, None]
    low = jnp.min(jnp.where(match, cols, blocks - 1), axis=1)
    high = jnp.max(jnp.where(match, cols, 0), axis=1)
    return jnp.stack([low, high], axis=1).reshape(-1).astype(jnp.int32)


def shared_slots(cols, blocks):
    tiles = jnp.arange(cols.shape[0])
    chip = cols // 2
    before = (chip[:, None] == chip[None, :]) & (tiles[None, :] < tiles[:, None])
    rank = jnp.sum(before.astype(jnp.int32), axis=1)
    device = 2 * chip + rank % 2
    slot = rank // 2
    entry = 1 + 2 * (tiles // 2) + (cols % 2 != rank % 2).astype(jnp.int32)
    place = device * SHARED + slot
    hit = (place[None, :] == jnp.arange(blocks * SHARED)[:, None]) & (slot[None, :] < SHARED)
    table = jnp.sum(jnp.where(hit, entry[None, :], 0), axis=1).astype(jnp.int32)
    level = sum((rank >= 2 * shared).astype(jnp.int32) for shared in CHOICES)
    return table.reshape(blocks, SHARED), jnp.max(level)


def message_picks(cols, mine, me, blocks):
    source = jnp.arange(blocks * SUB) // SUB
    kind = (jnp.arange(blocks * SUB) % SUB) // 2
    pair = cols.reshape(blocks, 2)
    own_pair = lax.dynamic_index_in_dim(pair, me, 0, keepdims=False)
    columns = jnp.concatenate([jnp.stack([me, me ^ 1]).astype(jnp.int32), own_pair])[:, None]
    first = jnp.repeat(pair[:, 0], SUB)
    second = jnp.repeat(pair[:, 1], SUB)
    named = jnp.where(kind == 1, source, jnp.where(kind == 2, first, second))
    column_hit = (named[None, :] == columns) & (kind > 0)[None, :]
    row_blocks = jnp.concatenate([me.reshape(1).astype(jnp.int32), (mine + 1) // 2 - 1])[:, None]
    row_hit = (source[None, :] == row_blocks) & (kind == 0)[None, :]
    hits = jnp.concatenate([column_hit, row_hit], axis=0).astype(jnp.bfloat16)
    return jnp.pad(hits, ((0, PICKS - hits.shape[0]), (0, 0)))


def pieces(x):
    rows, features = x.shape
    tiled = x.reshape(rows // SUB, SUB, features // LANES, LANES).transpose(0, 2, 1, 3)
    return tiled.reshape(-1, SUB, LANES)


def small_table(x):
    return pltpu.SMEM(x.shape, x.dtype), pltpu.SemaphoreType.DMA


def fetch(cols, spread, query_unit):
    blocks = lax.axis_size("dp")
    wanted = vmem_call(
        first_gather_kernel,
        pltpu.VMEM((blocks, 3 * SUB, LANES), jnp.bfloat16),
        0,
        2,
        small_table(cols),
        name="gather",
        n_any=1,
    )(cols, spread, pieces(query_unit))
    return exchange(wanted)


def general_path(query_emb, doc_emb, spread, cols, table, info, picks, own):
    qu, du, inv, _, et_own, _ = own
    fetched = fetch(cols, spread, qu)
    blocks = lax.axis_size("dp")
    rows, features = query_emb.shape
    row_tiles, col_tiles = rows // SUB, features // LANES
    sds = pltpu.VMEM
    bf16, f32 = jnp.bfloat16, jnp.float32
    send, et, row_total, dk = vmem_call(
        tiles_kernel,
        (
            sds((row_tiles, col_tiles, 5 * SUB, LANES), bf16),
            sds((2, rows, rows), f32),
            sds((1, rows), f32),
            sds((2, rows, features), bf16),
        ),
        0,
        3,
        name="tiles",
    )(qu, et_own, fetched)
    parts = exchange(send.reshape(blocks, 5 * SUB, LANES))
    acc = pltpu.VMEM((blocks, SUB, LANES), f32)
    combined = vmem_call(
        combine_kernel, sds((blocks, 2 * SUB, LANES), bf16), 1, 1, (acc, acc, acc), name="combine"
    )(cols, parts)
    home = exchange(combined)
    grad = jax.ShapeDtypeStruct((rows, features), f32)
    return vmem_call(final_kernel, (grad, grad), 0, 10, name="final")(
        query_emb, doc_emb, qu, du, inv, et_own, et, row_total, dk, home
    )


def short_path(shared, query_emb, doc_emb, spread, cols, table, info, picks, own):
    qu, du, inv, e_own, et_own, other = own
    fetched = fetch(cols, spread, qu)
    blocks = lax.axis_size("dp")
    rows, features = query_emb.shape
    assert rows == LANES
    sds = pltpu.VMEM
    bf16, f32 = jnp.bfloat16, jnp.float32
    wide = sds((rows, features), bf16)
    grad = jax.ShapeDtypeStruct((rows, features), f32)
    send, e, row_total, doc_units = vmem_call(
        row_side_kernel,
        (
            sds((blocks, (shared + 1) * SUB, LANES), bf16),
            sds((2, rows, rows), f32),
            sds((rows, 1), f32),
            sds((3 * rows, features), bf16),
        ),
        0,
        5,
        (pltpu.VMEM((SUB, LANES), bf16), *small_table(table)),
        name="rows",
        n_any=1,
    )(table, qu, du, e_own, et_own, fetched.reshape(3 * blocks, SUB, LANES))
    recv = exchange(send)
    acc, partner, sums = vmem_call(
        doc_side_kernel,
        (sds((rows, features), f32), wide, sds((PICKS, LANES), f32)),
        0,
        5,
        (
            pltpu.VMEM(((shared + 1) * rows, features), bf16),
            pltpu.VMEM((rows, features), bf16),
            pltpu.SemaphoreType.DMA,
            *small_table(info),
        ),
        name="docs",
        n_any=2,
    )(info, other, picks, qu, du, et_own, recv)
    swapped = swap_cores(partner)
    grad_scratch = (pltpu.VMEM((rows, features), f32), pltpu.SemaphoreType.DMA((2,)))
    grad_query = vmem_call(
        query_side_kernel, grad, 0, 7, grad_scratch, name="queries", out_space=pl.ANY
    )(sums, query_emb, inv, e_own, e, row_total, doc_units)
    grad_doc = vmem_call(
        doc_final_kernel, grad, 0, 4, grad_scratch, name="final", out_space=pl.ANY
    )(doc_emb, inv, acc, swapped)
    return grad_query, grad_doc


def swap_cores(x):
    return lax.ppermute(x, "dp", [(i, i ^ 1) for i in range(lax.axis_size("dp"))])


def on_device(query_emb, doc_emb, pair_blocks, active_pair_count):
    blocks = lax.axis_size("dp")
    me = lax.axis_index("dp")
    rows, features = query_emb.shape
    row_tiles, col_tiles = rows // SUB, features // LANES
    assert row_tiles * col_tiles == blocks

    spread = exchange(pieces(doc_emb))
    cols = row_columns(pair_blocks, active_pair_count, blocks)
    mat, wide = pltpu.VMEM((rows, rows), jnp.float32), pltpu.VMEM((rows, features), jnp.bfloat16)
    own = vmem_call(
        own_pair_kernel, (wide, wide, pltpu.VMEM((rows, 2), jnp.float32), mat, mat), 0, 2, name="own", keep=False
    )(query_emb, doc_emb)
    own = (*own, swap_cores(own[1]))
    table, choice = shared_slots(cols, blocks)
    info = lax.dynamic_index_in_dim(table, me, 0, keepdims=False)
    picks = message_picks(cols, info, me, blocks)
    table = jnp.pad(3 * (jnp.maximum(table - 1, 0) // 2) + 2, ((0, 0), (0, SUB - SHARED))).reshape(-1)
    info = jnp.pad(info, (0, LANES - SHARED))
    spread, cols, table, info, picks, choice, own = lax.optimization_barrier(
        (spread, cols, table, info, picks, choice, own)
    )
    args = (query_emb, doc_emb, spread, cols, table, info, picks, own)
    paths = [functools.partial(short_path, shared) for shared in CHOICES] + [general_path]
    return lax.switch(choice, paths, *args)


def solution(mesh):
    return jax.shard_map(
        on_device,
        mesh=mesh,
        in_specs=(P("dp", None), P("dp", None), P(), P()),
        out_specs=(P("dp", None), P("dp", None)),
        check_vma=False,
    )
```
